256 devices in a mesh: sec: 2 (over core), row: 16 (over y_hi, z), col: 8 (over y_lo, x).
Axes of the slice: x: 4, y: 4 (y_hi: 2, y_lo: 2; y = y_hi * 2 + y_lo), z: 8, core: 2. Of those that a mesh axis runs over, the one named last changes fastest.
Arguments:
- grid_terms: float32 [768, 1536, 128], P(('row', 'col'), 'sec'), may hold values from -6 to 6
- pair_orders: int32 [256], replicated, may hold values from 0 to 255, each once
- legendre: bfloat16 [256, 513, 768], P(('sec', 'row', 'col')), may hold values from -0.21875 to 0.21875
- state: bfloat16 [256, 513, 256], P(('sec', 'row', 'col')), may hold values from -6 to 6
- kappa: float32 [128], replicated, may hold values from 0.05 to 5
- right_op: bfloat16 [128, 128], replicated, may hold values from -0.5 to 0.5
- left_op: bfloat16 [128, 128], replicated, may hold values from -0.5 to 0.5
Outputs:
- evolved: float32 [768, 1536, 128], P(('row', 'col'), 'sec')
- new_state: bfloat16 [256, 513, 256], P(('sec', 'row', 'col'))
The draws below stay inside these ranges and needn't reach their ends.
Inputs may be any that keep to these rules, and one draw needn't show every extreme that they name: pair_orders is a permutation: each order below 256 is the lower order of exactly one pair.
All inputs are finite; a program needn't handle non-finite values.
Results may differ from the reference program's by a relative error of at most 0.0085.
Values may be sent and summed in bfloat16 or wider, within the bound.
A program may use at most 64 MiB of HBM per device.

```python
import math
import jax
import jax.numpy as jnp
from jax import lax

NTH = 768
NPH = 1536
NR = 128
L = 512
PAIRS = 256


def steps_of(rng, extent, shards, least, top_value):
    level = 1.0
    for axis_at, shards_of in shards:
        heights = jax.random.uniform(jax.random.fold_in(jax.random.fold_in(rng, 6), axis_at), (shards_of,), jnp.float32, least / len(shards), top_value / len(shards))
        level = level * jnp.repeat(jnp.exp(heights), extent[axis_at] // shards_of).reshape((-1,) + (1,) * (len(extent) - 1 - axis_at))
    return level


def centred(rng, dims, spread, most, cuts=(), held_as=jnp.bfloat16):
    level = steps_of(rng, dims, cuts, -0.22, 0.18) if cuts else 1.0
    result = jax.random.normal(rng, dims, jnp.float32) * spread * level
    return jnp.minimum(jnp.maximum(result, -most), most).astype(held_as)


def setup_inputs(seed: int = 0) -> dict:
    streams_of = jax.random.split(jax.random.key(seed), 8)
    return {
        "grid_terms": centred(streams_of[0], (NTH, NPH, NR), 1.0, 6.0, ((0, 128), (1, 2)), jnp.float32),
        "pair_orders": jax.random.permutation(streams_of[1], PAIRS).astype(jnp.int32),
        "legendre": centred(streams_of[2], (PAIRS, L + 1, NTH), NTH ** -0.5, 0.21875, ((0, 256),)),
        "state": centred(streams_of[3], (PAIRS, L + 1, 2 * NR), 1.0, 6.0, ((0, 256),)),
        "kappa": jnp.clip(jnp.exp(jax.random.uniform(streams_of[4], (NR,), jnp.float32, math.log(0.05), math.log(5.0))), 0.05, 5.0),
        "right_op": centred(streams_of[5], (NR, NR), NR ** -0.5, 0.5),
        "left_op": centred(streams_of[6], (NR, NR), NR ** -0.5, 0.5),
    }


time_step = 0.5
filter_strength = 36.0
filter_power = 36.0

def reference(grid_terms, pair_orders, legendre, state, kappa, right_op, left_op):
    pair_total = pair_orders.shape[0]
    degrees = 2 * pair_total
    latitudes = grid_terms.shape[0]
    longitudes = grid_terms.shape[1]
    radial = grid_terms.shape[2]
    orders = jnp.stack([pair_orders, degrees - 1 - pair_orders], axis=1).reshape(degrees)
    spectrum = jnp.fft.rfft(grid_terms, axis=1) / math.sqrt(longitudes)
    picked = jnp.take(spectrum, orders, axis=1)
    fourier = jnp.stack([jnp.real(picked), jnp.imag(picked)], axis=2)
    fourier = jnp.transpose(fourier, (1, 0, 2, 3)).reshape(degrees, latitudes, 2 * radial).astype(jnp.bfloat16)
    fourier = lax.optimization_barrier(fourier)
    paired_fourier = fourier.reshape(pair_total, 2, latitudes, 2 * radial)
    row_index = jnp.arange(degrees + 1, dtype=jnp.int32)
    radial_mode = jnp.arange(radial, dtype=jnp.int32).astype(jnp.float32) / radial
    damping = jnp.exp(-filter_strength * radial_mode ** filter_power)
    left_wide = left_op.astype(jnp.float32)
    right_wide = right_op.astype(jnp.float32)

    def one_pair(pieces):
        legend_rows, paired_rows, prior_state, low_order = pieces
        leading = row_index < degrees - low_order
        degree = jnp.where(leading, low_order + row_index, row_index - 1).astype(jnp.float32)
        legend_wide = legend_rows.astype(jnp.float32)
        both_orders = jnp.einsum('it,otx->iox', legend_wide, paired_rows.astype(jnp.float32))
        coefficient = jnp.where(leading[:, None], both_orders[:, 0], both_orders[:, 1])
        right_side = (prior_state.astype(jnp.float32) + time_step * coefficient).astype(jnp.bfloat16)
        right_side = lax.optimization_barrier(right_side).reshape(degrees + 1, 2, radial).astype(jnp.float32)
        eigen_part = jnp.einsum('icr,rk->ick', right_side, right_wide)
        degree_term = degree * (degree + 1.0) / (degrees * degrees)
        factor = damping[None, :] / (1.0 + kappa[None, :] + degree_term[:, None])
        scaled = (eigen_part * factor[:, None, :]).astype(jnp.bfloat16)
        scaled = lax.optimization_barrier(scaled).astype(jnp.float32)
        new_rows = jnp.einsum('ick,kr->icr', scaled, left_wide).astype(jnp.bfloat16).reshape(degrees + 1, 2 * radial)
        new_wide = lax.optimization_barrier(new_rows).astype(jnp.float32)
        split_rows = jnp.stack([jnp.where(leading[:, None], new_wide, 0.0), jnp.where(leading[:, None], 0.0, new_wide)], axis=0)
        synthesis = jnp.einsum('it,oix->otx', legend_wide, split_rows).astype(jnp.bfloat16)
        return (new_rows, synthesis)
    new_state, synthesis = lax.map(one_pair, (legendre, paired_fourier, state, pair_orders))
    values = synthesis.reshape(degrees, latitudes, 2, radial).astype(jnp.float32)
    doubled = jnp.where(orders == 0, 2.0, 1.0).astype(jnp.float32)[:, None, None]
    packed = lax.complex(values[:, :, 0] * doubled, values[:, :, 1] * doubled)
    spectrum_out = jnp.zeros((longitudes // 2 + 1, latitudes, radial), packed.dtype).at[orders].set(packed)
    evolved = jnp.fft.irfft(spectrum_out, n=longitudes, axis=0) * (longitudes / 2.0) / math.sqrt(longitudes)
    evolved = jnp.transpose(evolved, (1, 0, 2)).astype(jnp.float32)
    return (evolved, new_state)
```

```python
import functools
import math

import jax
import jax.numpy as jnp
from jax import lax
from jax.experimental import pallas as pl
from jax.experimental.pallas import tpu as pltpu
from jax.sharding import PartitionSpec as P

time_step = 0.5
filter_strength = 36.0
MESH = pl.DeviceIdType.MESH
F32 = jnp.float32
BF16 = jnp.bfloat16

LAT = 6
HALF = 768
NR = 128
PEERS = 128
DEG = 512
NTH = 768
GROUPS = 3 * PEERS
ROWS = 8 * GROUPS


def ring(count, k):
    return count // 2 + lax.div(k + 1, 2) * (1 - 2 * lax.rem(k, 2))


def peer_of(i, row, col):
    z, y, x = lax.rem(row, 8), 2 * lax.div(row, 8) + lax.div(col, 4), lax.rem(col, 4)
    z2 = lax.rem(z + ring(8, lax.rem(i, 8)), 8)
    x2 = lax.rem(x + ring(4, lax.rem(lax.div(i, 8), 4)), 4)
    y2 = lax.rem(y + ring(4, lax.div(i, 32)), 4)
    return 8 * lax.div(y2, 2) + z2, 4 * lax.rem(y2, 2) + x2


def wave(order, longitude):
    longitudes = 2 * HALF
    phase = order * longitude
    turns = jnp.round(phase * (1.0 / longitudes))
    angle = (phase - turns * longitudes) * (math.pi / longitudes)
    square = angle * angle
    sine = angle * (1.0 + square * (-1 / 6 + square * (1 / 120 + square * (-1 / 5040 + square * (1 / 362880)))))
    cosine = 1.0 + square * (
        -1 / 2 + square * (1 / 24 + square * (-1 / 720 + square * (1 / 40320 - square * (1 / 3628800))))
    )
    scale = 1.0 / math.sqrt(longitudes)
    return scale - (2.0 * scale) * sine * sine, (-2.0 * scale) * sine * cosine


def dot(a, b):
    return jnp.dot(a, b, preferred_element_type=F32)


def kernel(
    order_ref, orders_ref, kappa_ref, right_ref, left_ref, grid_hbm, legendre_hbm, state_hbm,
    evolved_ref, new_ref,
    grid, grid_out, grid_in, table, table_t, wide, pack_a, got_a, pack_b, got_b, legendre, legendre_t,
    state, columns, factor, part_out, part_in,
    load_sem, send_sem, recv_sem,
):
    sec, row, col = lax.axis_index("sec"), lax.axis_index("row"), lax.axis_index("col")
    me = 8 * row + col
    partner = (1 - sec, row, col)
    sign = (1 - 2 * sec).astype(F32)

    loads = [pltpu.make_async_copy(grid_hbm.at[t], grid.at[t], load_sem.at[t]) for t in range(LAT)]
    loads.append(pltpu.make_async_copy(legendre_hbm.at[0], legendre, load_sem.at[LAT]))
    loads.append(pltpu.make_async_copy(state_hbm.at[0], state, load_sem.at[LAT + 1]))
    for load in loads:
        load.start()

    barrier = pltpu.get_barrier_semaphore()

    def greet(i, _):
        row2, col2 = peer_of(i, row, col)
        pl.semaphore_signal(barrier, inc=1, device_id=(sec, row2, col2), device_id_type=MESH)
        return 0

    pl.semaphore_signal(barrier, inc=1, device_id=partner, device_id_type=MESH)
    lax.fori_loop(0, PEERS - 1, greet, 0)

    for t in range(LAT):
        loads[t].wait()
        grid_out[t] = grid[t].astype(BF16)

    low = orders_ref[pl.ds(sec, 1), :]
    even = jnp.where(lax.rem(low, 2) == 0, low, DEG - 1 - low).astype(F32)
    even_t = jnp.transpose(jnp.broadcast_to(even, (PEERS, PEERS)))

    pl.semaphore_wait(barrier, PEERS)

    def give(t):
        return pltpu.make_async_remote_copy(
            grid_out.at[t], grid_in.at[t], send_sem.at[t], recv_sem.at[t], device_id=partner, device_id_type=MESH
        )

    for t in range(LAT):
        give(t).start()

    for lane in range(HALF // 128):
        longitude = (lax.broadcasted_iota(jnp.int32, (PEERS, 128), 1) + 128 * lane).astype(F32)
        for parity in range(2):
            order = even_t if parity == 0 else (DEG - 1.0) - even_t
            real, imag = wave(order, longitude)
            if parity == 1:
                real, imag = real * sign, imag * sign
            span = pl.ds(128 * lane, 128)
            table[parity, 0:PEERS, span] = real.astype(BF16)
            table[parity, PEERS : 2 * PEERS, span] = imag.astype(BF16)

    for k in range(LAT // 2):
        give(2 * k).wait_recv()
        give(2 * k + 1).wait_recv()
        for parity in range(2):
            values = []
            for t in (2 * k, 2 * k + 1):
                other = grid_in[t].astype(F32)
                values.append((grid[t] + other if parity == 0 else grid[t] - other).astype(BF16))
            sums = dot(table[parity], jnp.concatenate(values, axis=1))
            for c in range(2):
                for j in range(2):
                    at = (2 * k + j) * 4 + 2 * parity + c
                    wide[pl.ds(at, PEERS, stride=24), :] = sums[c * PEERS : (c + 1) * PEERS, j * NR : (j + 1) * NR]
    for t in range(LAT):
        give(t).wait_send()

    def narrow(pack):
        def body(i, _):
            pack[pl.ds(32 * i, 32)] = wide[pl.ds(256 * i, 256), :].reshape(32, 8, NR).astype(BF16)
            return 0

        lax.fori_loop(0, GROUPS // 32, body, 0)

    def widen(got):
        def body(i, _):
            wide[pl.ds(256 * i, 256), :] = got[pl.ds(32 * i, 32)].astype(F32).reshape(256, NR)
            return 0

        lax.fori_loop(0, GROUPS // 32, body, 0)

    def exchange(pack, got, sem):
        def body(i, _):
            row2, col2 = peer_of(i, row, col)
            pltpu.make_async_remote_copy(
                pack.at[pl.ds(3 * (8 * row2 + col2), 3)], got.at[pl.ds(3 * me, 3)],
                send_sem.at[sem], recv_sem.at[sem], device_id=(sec, row2, col2), device_id_type=MESH,
            ).start()
            return 0

        lax.fori_loop(0, PEERS - 1, body, 0)
        got[pl.ds(3 * me, 3)] = pack[pl.ds(3 * me, 3)]

    def finish(pack, got, sem):
        count = 3 * (PEERS - 1)
        both = pltpu.make_async_remote_copy(
            pack.at[pl.ds(0, count)], got.at[pl.ds(0, count)], send_sem.at[sem], recv_sem.at[sem],
            device_id=partner, device_id_type=MESH,
        )
        both.wait_recv()
        both.wait_send()

    narrow(pack_a)
    exchange(pack_a, got_a, LAT)

    for lane in range(HALF // 128):
        longitude = (lax.broadcasted_iota(jnp.int32, (128, PEERS), 0) + 128 * lane).astype(F32)
        for parity in range(2):
            order = jnp.broadcast_to(even if parity == 0 else (DEG - 1.0) - even, (128, PEERS))
            real, imag = wave(order, longitude)
            if parity == 1:
                real, imag = real * sign, imag * sign
            span = pl.ds(128 * lane, 128)
            table_t[parity, span, 0:PEERS] = real.astype(BF16)
            table_t[parity, span, PEERS : 2 * PEERS] = imag.astype(BF16)
    loads[LAT].wait()
    loads[LAT + 1].wait()
    for i in range(4):
        for j in range(6):
            legendre_t[pl.ds(128 * j, 128), pl.ds(128 * i, 128)] = jnp.transpose(
                legendre[pl.ds(128 * i, 128), pl.ds(128 * j, 128)].astype(F32)
            ).astype(BF16)
    mine = order_ref[PEERS * sec + me]
    index = lax.broadcasted_iota(jnp.int32, (DEG + 1, NR), 0)
    leading = index < DEG - mine
    degree = jnp.where(leading, mine + index, index - 1).astype(F32)
    mode = lax.broadcasted_iota(jnp.int32, (1, NR), 1).astype(F32) * (1.0 / NR)
    mode4 = (mode * mode) * (mode * mode)
    mode8 = mode4 * mode4
    mode16 = mode8 * mode8
    damping = jnp.exp(-filter_strength * (mode16 * mode16 * mode4))
    factor[...] = damping / (1.0 + kappa_ref[...] + degree * (degree + 1.0) * (1.0 / (DEG * DEG)))

    finish(pack_a, got_a, LAT)

    widen(got_a)
    for q in range(4):
        columns[:, q * NR : (q + 1) * NR] = wide[pl.ds(q, NTH, stride=4), :].astype(BF16)
    both = dot(legendre[...], columns[...])
    index = lax.broadcasted_iota(jnp.int32, (DEG + 1, 2 * NR), 0)
    first = (index < DEG - mine) == (lax.rem(mine, 2) == 0)
    coefficient = jnp.where(first, both[:, : 2 * NR], both[:, 2 * NR :])
    right_side = (state[...].astype(F32) + time_step * coefficient).astype(BF16)
    parts = []
    for c in range(2):
        eigen = dot(right_side[:, c * NR : (c + 1) * NR], right_ref[...])
        scaled = (eigen * factor[...]).astype(BF16)
        parts.append(dot(scaled, left_ref[...]))
    new_wide = jnp.concatenate(parts, axis=1)
    new_ref[0] = new_wide.astype(BF16)
    new_wide = new_wide.astype(BF16).astype(F32)
    split = jnp.concatenate([jnp.where(first, new_wide, 0.0), jnp.where(first, 0.0, new_wide)], axis=1)
    tail = split[DEG:, :]
    main = split[:DEG, :].astype(BF16)
    ends = legendre[DEG:, :].astype(F32)
    tail_t = jnp.transpose(jnp.broadcast_to(ends, (128, NTH)))
    for q in range(4):
        span = slice(q * NR, (q + 1) * NR)
        wide[pl.ds(q, NTH, stride=4), :] = dot(legendre_t[...], main[:, span]) + tail_t * tail[:, span]
    narrow(pack_b)
    exchange(pack_b, got_b, LAT + 1)
    finish(pack_b, got_b, LAT + 1)
    widen(got_b)

    def pass_on(t):
        return pltpu.make_async_remote_copy(
            part_out.at[t], part_in.at[t], send_sem.at[LAT + 2 + t], recv_sem.at[LAT + 2 + t],
            device_id=partner, device_id_type=MESH,
        )

    for k in range(LAT // 2):
        sums = []
        for parity in range(2):
            halves = []
            for j in range(2):
                at = (2 * k + j) * 4 + 2 * parity
                halves.append(
                    jnp.concatenate(
                        [wide[pl.ds(at + c, PEERS, stride=24), :].astype(BF16) for c in range(2)], axis=0
                    )
                )
            sums.append(dot(table_t[parity], jnp.concatenate(halves, axis=1)))
        keep, other = sums[0] + sums[1], (sums[0] - sums[1]).astype(BF16)
        for j in range(2):
            t = 2 * k + j
            evolved_ref[t] = keep[:, j * NR : (j + 1) * NR]
            part_out[t] = other[:, j * NR : (j + 1) * NR]
            pass_on(t).start()
    for t in range(LAT):
        pass_on(t).wait_recv()
        evolved_ref[t] = evolved_ref[t] + part_in[t].astype(F32)
    for t in range(LAT):
        pass_on(t).wait_send()


def on_device(grid_terms, pair_orders, legendre, state, kappa, right_op, left_op):
    vmem = pl.BlockSpec(memory_space=pltpu.VMEM)
    anywhere = pl.BlockSpec(memory_space=pl.ANY)
    smem = pl.BlockSpec(memory_space=pltpu.SMEM)
    sems = 2 * LAT + 2
    evolved, new_state = pl.pallas_call(
        kernel,
        out_shape=(
            jax.ShapeDtypeStruct((LAT, HALF, NR), F32),
            jax.ShapeDtypeStruct((1, DEG + 1, 2 * NR), BF16),
        ),
        in_specs=[smem, vmem, vmem, vmem, vmem, anywhere, anywhere, anywhere],
        out_specs=(vmem, vmem),
        scratch_shapes=[
            pltpu.VMEM((LAT, HALF, NR), F32),
            pltpu.VMEM((LAT, HALF, NR), BF16),
            pltpu.VMEM((LAT, HALF, NR), BF16),
            pltpu.VMEM((2, 2 * PEERS, HALF), BF16),
            pltpu.VMEM((2, HALF, 2 * PEERS), BF16),
            pltpu.VMEM((ROWS, NR), F32),
            pltpu.VMEM((GROUPS, 8, NR), BF16),
            pltpu.VMEM((GROUPS, 8, NR), BF16),
            pltpu.VMEM((GROUPS, 8, NR), BF16),
            pltpu.VMEM((GROUPS, 8, NR), BF16),
            pltpu.VMEM((DEG + 1, NTH), BF16),
            pltpu.VMEM((NTH, DEG), BF16),
            pltpu.VMEM((DEG + 1, 2 * NR), BF16),
            pltpu.VMEM((NTH, 4 * NR), BF16),
            pltpu.VMEM((DEG + 1, NR), F32),
            pltpu.VMEM((LAT, HALF, NR), BF16),
            pltpu.VMEM((LAT, HALF, NR), BF16),
            pltpu.SemaphoreType.DMA((LAT + 2,)),
            pltpu.SemaphoreType.DMA((sems,)),
            pltpu.SemaphoreType.DMA((sems,)),
        ],
        compiler_params=pltpu.CompilerParams(
            collective_id=0, has_side_effects=True, vmem_limit_bytes=60 * 1024 * 1024
        ),
    )(
        pair_orders,
        pair_orders.reshape(2, PEERS),
        kappa.reshape(1, NR),
        right_op,
        left_op,
        grid_terms,
        legendre,
        state,
    )
    return evolved, new_state


def solution(mesh):
    return jax.shard_map(
        on_device,
        mesh=mesh,
        in_specs=(
            P(("row", "col"), "sec", None),
            P(),
            P(("sec", "row", "col"), None, None),
            P(("sec", "row", "col"), None, None),
            P(),
            P(),
            P(),
        ),
        out_specs=(P(("row", "col"), "sec", None), P(("sec", "row", "col"), None, None)),
        check_vma=False,
    )
```

```python
import functools
import math

import jax
import jax.numpy as jnp
from jax import lax
from jax.experimental import pallas as pl
from jax.experimental.pallas import tpu as pltpu
from jax.sharding import PartitionSpec as P

time_step = 0.5
filter_strength = 36.0
MESH = pl.DeviceIdType.MESH
F32 = jnp.float32
BF16 = jnp.bfloat16

LAT = 6
HALF = 768
NR = 128
PEERS = 128
DEG = 512
NTH = 768


def ring(count, k):
    return count // 2 + lax.div(k + 1, 2) * (1 - 2 * lax.rem(k, 2))


def peer_of(i, row, col):
    z, y, x = lax.rem(row, 8), 2 * lax.div(row, 8) + lax.div(col, 4), lax.rem(col, 4)
    z2 = lax.rem(z + ring(8, lax.rem(i, 8)), 8)
    x2 = lax.rem(x + ring(4, lax.rem(lax.div(i, 8), 4)), 4)
    y2 = lax.rem(y + ring(4, lax.div(i, 32)), 4)
    return 8 * lax.div(y2, 2) + z2, 4 * lax.rem(y2, 2) + x2


def wave(order, longitude):
    longitudes = 2 * HALF
    phase = order * longitude
    turns = jnp.round(phase * (1.0 / longitudes))
    angle = (phase - turns * longitudes) * (math.pi / longitudes)
    square = angle * angle
    sine = angle * (1.0 + square * (-1 / 6 + square * (1 / 120 + square * (-1 / 5040 + square * (1 / 362880)))))
    cosine = 1.0 + square * (
        -1 / 2 + square * (1 / 24 + square * (-1 / 720 + square * (1 / 40320 - square * (1 / 3628800))))
    )
    scale = 1.0 / math.sqrt(longitudes)
    return scale - (2.0 * scale) * sine * sine, (-2.0 * scale) * sine * cosine


def dot(a, b):
    return jnp.dot(a, b, preferred_element_type=F32)


def kernel(
    orders_hbm, kappa_hbm, right_hbm, left_hbm, grid_hbm, legendre_hbm, state_hbm,
    keep_ref, part_in, new_ref,
    orders_s, orders_v, kappa, right, left,
    grid, grid_out, grid_in, table, table_t,
    wide_a0, wide_a1, wide_b0, wide_b1, pack_a0, pack_a1, pack_b0, pack_b1, got_a0, got_a1, got_b0, got_b1,
    legendre, permute, rows, rows_t, state, columns, factor, part_out,
    load_sem, send_sem, recv_sem,
):
    sec, row, col = lax.axis_index("sec"), lax.axis_index("row"), lax.axis_index("col")
    me = 8 * row + col
    partner = (1 - sec, row, col)
    sign = (1 - 2 * sec).astype(F32)

    loads = [pltpu.make_async_copy(grid_hbm.at[t], grid.at[t], load_sem.at[t]) for t in range(LAT)]
    for source, target in (
        (orders_hbm, orders_v), (orders_hbm, orders_s), (legendre_hbm.at[0], legendre), (state_hbm.at[0], state),
        (kappa_hbm, kappa), (right_hbm, right), (left_hbm, left),
    ):
        loads.append(pltpu.make_async_copy(source, target, load_sem.at[len(loads)]))
    for load in loads:
        load.start()

    barrier = pltpu.get_barrier_semaphore()

    def greet(i, _):
        row2, col2 = peer_of(i, row, col)
        pl.semaphore_signal(barrier, inc=1, device_id=(sec, row2, col2), device_id_type=MESH)
        return 0

    pl.semaphore_signal(barrier, inc=1, device_id=partner, device_id_type=MESH)
    lax.fori_loop(0, PEERS - 1, greet, 0)

    for t in range(LAT):
        loads[t].wait()
        grid_out[t] = grid[t].astype(BF16)

    loads[LAT].wait()
    low = orders_v[pl.ds(sec, 1), :]
    even = jnp.where(lax.rem(low, 2) == 0, low, DEG - 1 - low).astype(F32)
    even_t = jnp.transpose(jnp.broadcast_to(even, (PEERS, PEERS)))

    pl.semaphore_wait(barrier, PEERS)

    def give(t):
        return pltpu.make_async_remote_copy(
            grid_out.at[t], grid_in.at[t], send_sem.at[t], recv_sem.at[t], device_id=partner, device_id_type=MESH
        )

    for t in range(LAT):
        give(t).start()

    for lane in range(HALF // 128):
        longitude = (lax.broadcasted_iota(jnp.int32, (PEERS, 128), 1) + 128 * lane).astype(F32)
        for parity in range(2):
            order = even_t if parity == 0 else (DEG - 1.0) - even_t
            real, imag = wave(order, longitude)
            if parity == 1:
                real, imag = real * sign, imag * sign
            span = pl.ds(128 * lane, 128)
            table[parity, 0:PEERS, span] = real.astype(BF16)
            table[parity, PEERS : 2 * PEERS, span] = imag.astype(BF16)

    def there(c, parity, t):
        at = 12 * c + 6 * parity + t
        return (wide_a0, pl.ds(at, PEERS, stride=16)) if at < 16 else (wide_a1, pl.ds(at - 16, PEERS, stride=8))

    def back(c, parity, t):
        at = 12 * c + 6 * parity + t
        return (wide_b0, pl.ds(at, PEERS, stride=8)) if at < 8 else (wide_b1, pl.ds(at - 8, PEERS, stride=16))

    for k in range(LAT // 2):
        give(2 * k).wait_recv()
        give(2 * k + 1).wait_recv()
        for parity in range(2):
            values = []
            for t in (2 * k, 2 * k + 1):
                other = grid_in[t].astype(F32)
                values.append((grid[t] + other if parity == 0 else grid[t] - other).astype(BF16))
            sums = dot(table[parity], jnp.concatenate(values, axis=1))
            for c in range(2):
                for j in range(2):
                    wide, span = there(c, parity, 2 * k + j)
                    wide[span, :] = sums[c * PEERS : (c + 1) * PEERS, j * NR : (j + 1) * NR]
    for t in range(LAT):
        give(t).wait_send()

    def narrow(wide, pack):
        def body(i, _):
            pack[pl.ds(32 * i, 32)] = wide[pl.ds(256 * i, 256), :].reshape(32, 8, NR).astype(BF16)
            return 0

        lax.fori_loop(0, pack.shape[0] // 32, body, 0)

    def widen(got, wide):
        def body(i, _):
            wide[pl.ds(256 * i, 256), :] = got[pl.ds(32 * i, 32)].astype(F32).reshape(256, NR)
            return 0

        lax.fori_loop(0, got.shape[0] // 32, body, 0)

    def exchange(pack, got, sem):
        tiles = pack.shape[0] // PEERS

        def body(i, _):
            row2, col2 = peer_of(i, row, col)
            pltpu.make_async_remote_copy(
                pack.at[pl.ds(tiles * (8 * row2 + col2), tiles)], got.at[pl.ds(tiles * me, tiles)],
                send_sem.at[sem], recv_sem.at[sem], device_id=(sec, row2, col2), device_id_type=MESH,
            ).start()
            return 0

        lax.fori_loop(0, PEERS - 1, body, 0)
        got[pl.ds(tiles * me, tiles)] = pack[pl.ds(tiles * me, tiles)]

    def whole(pack, got, sem):
        count = pack.shape[0] // PEERS * (PEERS - 1)
        return pltpu.make_async_remote_copy(
            pack.at[pl.ds(0, count)], got.at[pl.ds(0, count)], send_sem.at[sem], recv_sem.at[sem],
            device_id=partner, device_id_type=MESH,
        )

    narrow(wide_a0, pack_a0)
    exchange(pack_a0, got_a0, LAT)
    narrow(wide_a1, pack_a1)
    exchange(pack_a1, got_a1, LAT + 1)

    for load in loads[LAT + 1 :]:
        load.wait()
    for lane in range(HALF // 128):
        longitude = (lax.broadcasted_iota(jnp.int32, (128, PEERS), 0) + 128 * lane).astype(F32)
        for parity in range(2):
            order = jnp.broadcast_to(even if parity == 0 else (DEG - 1.0) - even, (128, PEERS))
            real, imag = wave(order, longitude)
            if parity == 1:
                real, imag = real * sign, imag * sign
            span = pl.ds(128 * lane, 128)
            table_t[parity, span, 0:PEERS] = real.astype(BF16)
            table_t[parity, span, PEERS : 2 * PEERS] = imag.astype(BF16)
    for t in range(LAT):
        latitude = lax.broadcasted_iota(jnp.int32, (NTH, PEERS), 0)
        device = lax.broadcasted_iota(jnp.int32, (NTH, PEERS), 1)
        permute[:, t * PEERS : (t + 1) * PEERS] = jnp.where(latitude == LAT * device + t, 1.0, 0.0).astype(BF16)
    rows[...] = dot(legendre[...], permute[...]).astype(BF16)
    for i in range(4):
        for j in range(LAT):
            rows_t[pl.ds(128 * j, 128), pl.ds(128 * i, 128)] = jnp.transpose(
                rows[pl.ds(128 * i, 128), pl.ds(128 * j, 128)].astype(F32)
            ).astype(BF16)
    mine = orders_s[sec, me]
    index = lax.broadcasted_iota(jnp.int32, (DEG + 1, NR), 0)
    leading = index < DEG - mine
    first = leading == (lax.rem(mine, 2) == 0)
    degree = jnp.where(leading, mine + index, index - 1).astype(F32)
    mode = lax.broadcasted_iota(jnp.int32, (1, NR), 1).astype(F32) * (1.0 / NR)
    mode4 = (mode * mode) * (mode * mode)
    mode8 = mode4 * mode4
    mode16 = mode8 * mode8
    damping = jnp.exp(-filter_strength * (mode16 * mode16 * mode4))
    factor[...] = damping / (1.0 + kappa[...] + degree * (degree + 1.0) * (1.0 / (DEG * DEG)))

    for c in range(2):
        if c == 0:
            whole(pack_a0, got_a0, LAT).wait_recv()
            widen(got_a0, wide_a0)
        else:
            whole(pack_a1, got_a1, LAT + 1).wait_recv()
            widen(got_a1, wide_a1)
        for parity in range(2):
            for t in range(LAT):
                wide, span = there(c, parity, t)
                columns[t * PEERS : (t + 1) * PEERS, parity * NR : (parity + 1) * NR] = wide[span, :].astype(BF16)
        both = dot(rows[...], columns[...])
        coefficient = jnp.where(first, both[:, :NR], both[:, NR:])
        right_side = state[:, c * NR : (c + 1) * NR].astype(F32) + time_step * coefficient
        scaled = (dot(right_side.astype(BF16), right[...]) * factor[...]).astype(BF16)
        new = dot(scaled, left[...]).astype(BF16)
        new_ref[0, :, c * NR : (c + 1) * NR] = new
        new = new.astype(F32)
        split = jnp.concatenate([jnp.where(first, new, 0.0), jnp.where(first, 0.0, new)], axis=1)
        tail = split[DEG:, :]
        ends = jnp.transpose(jnp.broadcast_to(rows[DEG:, :].astype(F32), (128, NTH)))
        ends = jnp.concatenate([ends, ends], axis=1)
        sums = dot(rows_t[...], split[:DEG, :].astype(BF16)) + ends * tail
        for parity in range(2):
            for t in range(LAT):
                wide, span = back(c, parity, t)
                wide[span, :] = sums[t * PEERS : (t + 1) * PEERS, parity * NR : (parity + 1) * NR]
        if c == 0:
            narrow(wide_b0, pack_b0)
            exchange(pack_b0, got_b0, LAT + 2)
        else:
            narrow(wide_b1, pack_b1)
            exchange(pack_b1, got_b1, LAT + 3)

    whole(pack_a0, got_a0, LAT).wait_send()
    whole(pack_a1, got_a1, LAT + 1).wait_send()
    whole(pack_b0, got_b0, LAT + 2).wait_recv()
    widen(got_b0, wide_b0)
    whole(pack_b1, got_b1, LAT + 3).wait_recv()
    widen(got_b1, wide_b1)

    def pass_on(t):
        return pltpu.make_async_remote_copy(
            part_out.at[t], part_in.at[t], send_sem.at[LAT + 4 + t], recv_sem.at[LAT + 4 + t],
            device_id=partner, device_id_type=MESH,
        )

    for k in range(LAT // 2):
        sums = []
        for parity in range(2):
            halves = []
            for t in (2 * k, 2 * k + 1):
                pieces = []
                for c in range(2):
                    wide, span = back(c, parity, t)
                    pieces.append(wide[span, :].astype(BF16))
                halves.append(jnp.concatenate(pieces, axis=0))
            sums.append(dot(table_t[parity], jnp.concatenate(halves, axis=1)))
        keep, other = sums[0] + sums[1], (sums[0] - sums[1]).astype(BF16)
        for j in range(2):
            t = 2 * k + j
            part_out[t] = other[:, j * NR : (j + 1) * NR]
            pass_on(t).start()
            keep_ref[t] = keep[:, j * NR : (j + 1) * NR]
    for t in range(LAT):
        pass_on(t).wait_recv()
    whole(pack_b0, got_b0, LAT + 2).wait_send()
    whole(pack_b1, got_b1, LAT + 3).wait_send()
    for t in range(LAT):
        pass_on(t).wait_send()


def join(keep_ref, part_ref, new_ref, evolved_hbm, new_hbm, total, sem):
    copies = [pltpu.make_async_copy(new_ref, new_hbm, sem.at[LAT])]
    copies[0].start()
    for t in range(LAT):
        total[t] = keep_ref[t] + part_ref[t].astype(F32)
        copies.append(pltpu.make_async_copy(total.at[t], evolved_hbm.at[t], sem.at[t]))
        copies[-1].start()
    for copy in copies:
        copy.wait()


def on_device(grid_terms, pair_orders, legendre, state, kappa, right_op, left_op):
    vmem = pl.BlockSpec(memory_space=pltpu.VMEM)
    hbm = pl.BlockSpec(memory_space=pltpu.HBM)
    sems = 2 * LAT + 4
    mib = 1024 * 1024
    grid_shape = (LAT, HALF, NR)
    keep, part, new_state = pl.pallas_call(
        kernel,
        out_shape=(
            jax.ShapeDtypeStruct(grid_shape, F32),
            jax.ShapeDtypeStruct(grid_shape, BF16),
            jax.ShapeDtypeStruct((1, DEG + 1, 2 * NR), BF16),
        ),
        in_specs=[hbm] * 7,
        out_specs=(vmem, vmem, vmem),
        scratch_shapes=[
            pltpu.SMEM((2, PEERS), jnp.int32),
            pltpu.VMEM((2, PEERS), jnp.int32),
            pltpu.VMEM((1, NR), F32),
            pltpu.VMEM((NR, NR), BF16),
            pltpu.VMEM((NR, NR), BF16),
            pltpu.VMEM(grid_shape, F32),
            pltpu.VMEM(grid_shape, BF16),
            pltpu.VMEM(grid_shape, BF16),
            pltpu.VMEM((2, 2 * PEERS, HALF), BF16),
            pltpu.VMEM((2, HALF, 2 * PEERS), BF16),
        ]
        + [pltpu.VMEM((rows * PEERS, NR), F32) for rows in (16, 8, 8, 16)]
        + [pltpu.VMEM((tiles * PEERS, 8, NR), BF16) for tiles in (2, 1, 1, 2)] * 2
        + [
            pltpu.VMEM((DEG + 1, NTH), BF16),
            pltpu.VMEM((NTH, NTH), BF16),
            pltpu.VMEM((DEG + 1, NTH), BF16),
            pltpu.VMEM((NTH, DEG), BF16),
            pltpu.VMEM((DEG + 1, 2 * NR), BF16),
            pltpu.VMEM((NTH, 2 * NR), BF16),
            pltpu.VMEM((DEG + 1, NR), F32),
            pltpu.VMEM(grid_shape, BF16),
            pltpu.SemaphoreType.DMA((LAT + 7,)),
            pltpu.SemaphoreType.DMA((sems,)),
            pltpu.SemaphoreType.DMA((sems,)),
        ],
        compiler_params=pltpu.CompilerParams(collective_id=0, has_side_effects=True, vmem_limit_bytes=36 * mib),
    )(
        *(
            pltpu.with_memory_space_constraint(array, pltpu.HBM)
            for array in (
                pair_orders.reshape(2, PEERS), kappa.reshape(1, NR), right_op, left_op, grid_terms, legendre, state,
            )
        )
    )
    return pl.pallas_call(
        join,
        out_shape=(
            jax.ShapeDtypeStruct(grid_shape, F32),
            jax.ShapeDtypeStruct((1, DEG + 1, 2 * NR), BF16),
        ),
        in_specs=[vmem, vmem, vmem],
        out_specs=(hbm, hbm),
        scratch_shapes=[pltpu.VMEM(grid_shape, F32), pltpu.SemaphoreType.DMA((LAT + 1,))],
        compiler_params=pltpu.CompilerParams(vmem_limit_bytes=16 * mib),
    )(keep, part, new_state)


def solution(mesh):
    return jax.shard_map(
        on_device,
        mesh=mesh,
        in_specs=(
            P(("row", "col"), "sec", None),
            P(),
            P(("sec", "row", "col"), None, None),
            P(("sec", "row", "col"), None, None),
            P(),
            P(),
            P(),
        ),
        out_specs=(P(("row", "col"), "sec", None), P(("sec", "row", "col"), None, None)),
        check_vma=False,
    )
```

```python
import functools
import math

import jax
import jax.numpy as jnp
from jax import lax
from jax.experimental import pallas as pl
from jax.experimental.pallas import tpu as pltpu
from jax.sharding import PartitionSpec as P

time_step = 0.5
filter_strength = 36.0
MESH = pl.DeviceIdType.MESH
F32 = jnp.float32
BF16 = jnp.bfloat16

LAT = 6
HALF = 768
NR = 128
PEERS = 128
DEG = 512
NTH = 768


def ring(count, k):
    return count // 2 + lax.div(k + 1, 2) * (1 - 2 * lax.rem(k, 2))


def peer_of(i, row, col):
    z, y, x = lax.rem(row, 8), 2 * lax.div(row, 8) + lax.div(col, 4), lax.rem(col, 4)
    z2 = lax.rem(z + ring(8, lax.rem(i, 8)), 8)
    x2 = lax.rem(x + ring(4, lax.rem(lax.div(i, 8), 4)), 4)
    y2 = lax.rem(y + ring(4, lax.div(i, 32)), 4)
    return 8 * lax.div(y2, 2) + z2, 4 * lax.rem(y2, 2) + x2


def wave(order, longitude):
    longitudes = 2 * HALF
    phase = order * longitude
    turns = jnp.round(phase * (1.0 / longitudes))
    angle = (phase - turns * longitudes) * (math.pi / longitudes)
    square = angle * angle
    sine = angle * (1.0 + square * (-1 / 6 + square * (1 / 120 + square * (-1 / 5040 + square * (1 / 362880)))))
    cosine = 1.0 + square * (
        -1 / 2 + square * (1 / 24 + square * (-1 / 720 + square * (1 / 40320 - square * (1 / 3628800))))
    )
    scale = 1.0 / math.sqrt(longitudes)
    return scale - (2.0 * scale) * sine * sine, (-2.0 * scale) * sine * cosine


def dot(a, b):
    return jnp.dot(a, b, preferred_element_type=F32)


def kernel(
    orders_hbm, kappa_hbm, right_hbm, left_hbm, grid_hbm, legendre_hbm, state_hbm,
    sum_ref, table_other, passed_b0, passed_b1, new_ref,
    orders_s, orders_v, kappa, right, left,
    grid, grid_low, table, table_t,
    wide_a0, wide_a1, wide_b0, wide_b1, pack_a0, pack_a1, pack_b0, pack_b1, got_a0, got_a1, got_b0, got_b1,
    give_a0, give_a1, taken_a0, taken_a1,
    legendre, permute, rows, rows_t, state, columns, factor,
    load_sem, send_sem, recv_sem,
):
    sec, row, col = lax.axis_index("sec"), lax.axis_index("row"), lax.axis_index("col")
    me = 8 * row + col
    partner = (1 - sec, row, col)
    sign = (1 - 2 * sec).astype(F32)

    loads = [pltpu.make_async_copy(orders_hbm, orders_v, load_sem.at[0])]
    loads += [pltpu.make_async_copy(grid_hbm.at[t], grid.at[t], load_sem.at[t + 1]) for t in range(LAT)]
    for source, target in (
        (orders_hbm, orders_s), (legendre_hbm.at[0], legendre), (state_hbm.at[0], state),
        (kappa_hbm, kappa), (right_hbm, right), (left_hbm, left),
    ):
        loads.append(pltpu.make_async_copy(source, target, load_sem.at[len(loads)]))
    for load in loads:
        load.start()

    barrier = pltpu.get_barrier_semaphore()

    def greet(i, _):
        row2, col2 = peer_of(i, row, col)
        pl.semaphore_signal(barrier, inc=1, device_id=(sec, row2, col2), device_id_type=MESH)
        return 0

    pl.semaphore_signal(barrier, inc=1, device_id=partner, device_id_type=MESH)
    lax.fori_loop(0, PEERS - 1, greet, 0)

    loads[0].wait()
    evens = []
    for which in range(2):
        low = orders_v[pl.ds(sec if which == 0 else 1 - sec, 1), :]
        evens.append(jnp.where(lax.rem(low, 2) == 0, low, DEG - 1 - low).astype(F32))

    for which in range(2):
        even_t = jnp.transpose(jnp.broadcast_to(evens[which], (PEERS, PEERS)))
        real, imag = wave(even_t, lax.broadcasted_iota(jnp.int32, (PEERS, 128), 1).astype(F32))
        turn_real, turn_imag = wave(even_t, 128.0)
        turn_real, turn_imag = turn_real * math.sqrt(2 * HALF), turn_imag * math.sqrt(2 * HALF)
        for lane in range(HALF // 128):
            longitude = (lax.broadcasted_iota(jnp.int32, (8, 128), 1) + 128 * lane).astype(F32)
            last_real, last_imag = wave(jnp.full((8, 128), DEG - 1.0, F32), longitude)
            last_real = (last_real * (sign * math.sqrt(2 * HALF)))[:1]
            last_imag = (last_imag * (sign * math.sqrt(2 * HALF)))[:1]
            span = pl.ds(128 * lane, 128)
            table[which, 0:PEERS, span] = real.astype(BF16)
            table[which, PEERS : 2 * PEERS, span] = imag.astype(BF16)
            table[which, 2 * PEERS : 3 * PEERS, span] = (last_real * real + last_imag * imag).astype(BF16)
            table[which, 3 * PEERS :, span] = (last_imag * real - last_real * imag).astype(BF16)
            real, imag = real * turn_real - imag * turn_imag, imag * turn_real + real * turn_imag

    def there(c, parity, t):
        at = 12 * c + 6 * parity + t
        return (wide_a0, pl.ds(at, PEERS, stride=16)) if at < 16 else (wide_a1, pl.ds(at - 16, PEERS, stride=8))

    def narrow(wide, pack, added=None):
        def body(i, _):
            values = wide[pl.ds(256 * i, 256), :].reshape(32, 8, NR)
            if added is not None:
                values = values + added[pl.ds(32 * i, 32)].astype(F32)
            pack[pl.ds(32 * i, 32)] = values.astype(BF16)
            return 0

        lax.fori_loop(0, pack.shape[0] // 32, body, 0)

    for t in range(LAT):
        loads[t + 1].wait()
        grid_low[t] = grid[t].astype(BF16)
    for which in (1, 0):
        for k in range(LAT // 2):
            values = jnp.concatenate([grid_low[2 * k], grid_low[2 * k + 1]], axis=1)
            sums = dot(table[which], values)
            for parity in range(2):
                for c in range(2):
                    for j in range(2):
                        wide, span = there(c, parity, 2 * k + j)
                        at = (2 * parity + c) * PEERS
                        wide[span, :] = sums[at : at + PEERS, j * NR : (j + 1) * NR]
        if which == 1:
            narrow(wide_a0, give_a0)
            narrow(wide_a1, give_a1)

    pl.semaphore_wait(barrier, PEERS)

    def to_partner(source, target, sem):
        return pltpu.make_async_remote_copy(
            source, target, send_sem.at[sem], recv_sem.at[sem], device_id=partner, device_id_type=MESH
        )

    to_partner(give_a0, taken_a0, 0).start()
    to_partner(give_a1, taken_a1, 1).start()

    def exchange(pack, got, sem, start=0, stop=PEERS - 1):
        tiles = pack.shape[0] // PEERS

        def body(i, _):
            row2, col2 = peer_of(i, row, col)
            pltpu.make_async_remote_copy(
                pack.at[pl.ds(tiles * (8 * row2 + col2), tiles)], got.at[pl.ds(tiles * me, tiles)],
                send_sem.at[sem], recv_sem.at[sem], device_id=(sec, row2, col2), device_id_type=MESH,
            ).start()
            return 0

        lax.fori_loop(start, stop, body, 0)
        if stop == PEERS - 1:
            got[pl.ds(tiles * me, tiles)] = pack[pl.ds(tiles * me, tiles)]

    def whole(pack, got, sem, messages=PEERS - 1):
        count = pack.shape[0] // PEERS * messages
        return to_partner(pack.at[pl.ds(0, count)], got.at[pl.ds(0, count)], sem)

    to_partner(give_a0, taken_a0, 0).wait_recv()
    narrow(wide_a0, pack_a0, taken_a0)
    exchange(pack_a0, got_a0, 2)
    to_partner(give_a1, taken_a1, 1).wait_recv()
    narrow(wide_a1, pack_a1, taken_a1)
    exchange(pack_a1, got_a1, 3)

    for load in loads[LAT + 1 :]:
        load.wait()
    for lane in range(HALF // 128):
        longitude = (lax.broadcasted_iota(jnp.int32, (128, PEERS), 0) + 128 * lane).astype(F32)
        span = pl.ds(128 * lane, 128)
        for which in range(2):
            for parity in range(2):
                order = evens[which] if parity == 0 else (DEG - 1.0) - evens[which]
                real, imag = wave(jnp.broadcast_to(order, (128, PEERS)), longitude)
                if parity == 1:
                    real, imag = real * sign, imag * sign
                target = table_t if which == 0 else table_other
                at = 2 * PEERS * parity
                target[span, at : at + PEERS] = real.astype(BF16)
                target[span, at + PEERS : at + 2 * PEERS] = imag.astype(BF16)
    for t in range(LAT):
        latitude = lax.broadcasted_iota(jnp.int32, (NTH, PEERS), 0)
        device = lax.broadcasted_iota(jnp.int32, (NTH, PEERS), 1)
        permute[:, t * PEERS : (t + 1) * PEERS] = jnp.where(latitude == LAT * device + t, 1.0, 0.0).astype(BF16)
    rows[...] = dot(legendre[...], permute[...]).astype(BF16)
    for i in range(4):
        for j in range(LAT):
            rows_t[pl.ds(128 * j, 128), pl.ds(128 * i, 128)] = jnp.transpose(
                rows[pl.ds(128 * i, 128), pl.ds(128 * j, 128)].astype(F32)
            ).astype(BF16)
    mine = orders_s[sec, me]
    index = lax.broadcasted_iota(jnp.int32, (DEG + 1, NR), 0)
    leading = index < DEG - mine
    first = leading == (lax.rem(mine, 2) == 0)
    degree = jnp.where(leading, mine + index, index - 1).astype(F32)
    mode = lax.broadcasted_iota(jnp.int32, (1, NR), 1).astype(F32) * (1.0 / NR)
    mode4 = (mode * mode) * (mode * mode)
    mode8 = mode4 * mode4
    mode16 = mode8 * mode8
    damping = jnp.exp(-filter_strength * (mode16 * mode16 * mode4))
    factor[...] = damping / (1.0 + kappa[...] + degree * (degree + 1.0) * (1.0 / (DEG * DEG)))

    for c in range(2):
        if c == 0:
            whole(pack_a0, got_a0, 2).wait_recv()
            widen(got_a0, wide_a0)
        else:
            whole(pack_a1, got_a1, 3).wait_recv()
            widen(got_a1, wide_a1)
        for parity in range(2):
            for t in range(LAT):
                wide, span = there(c, parity, t)
                columns[t * PEERS : (t + 1) * PEERS, parity * NR : (parity + 1) * NR] = wide[span, :].astype(BF16)
        both = dot(rows[...], columns[...])
        coefficient = jnp.where(first, both[:, :NR], both[:, NR:])
        right_side = state[:, c * NR : (c + 1) * NR].astype(F32) + time_step * coefficient
        scaled = (dot(right_side.astype(BF16), right[...]) * factor[...]).astype(BF16)
        new = dot(scaled, left[...]).astype(BF16)
        new_ref[0, :, c * NR : (c + 1) * NR] = new
        new = new.astype(F32)
        split = jnp.concatenate([jnp.where(first, new, 0.0), jnp.where(first, 0.0, new)], axis=1)
        tail = split[DEG:, :]
        ends = jnp.transpose(jnp.broadcast_to(rows[DEG:, :].astype(F32), (128, NTH)))
        ends = jnp.concatenate([ends, ends], axis=1)
        sums = dot(rows_t[...], split[:DEG, :].astype(BF16)) + ends * tail
        for parity in range(2):
            for t in range(LAT):
                wide, span = back(wide_b0, wide_b1, c, parity, t)
                wide[span, :] = sums[t * PEERS : (t + 1) * PEERS, parity * NR : (parity + 1) * NR]
        if c == 0:
            narrow(wide_b0, pack_b0)
            exchange(pack_b0, got_b0, 4)
        else:
            narrow(wide_b1, pack_b1)
            for b in range(4):
                exchange(pack_b1, got_b1, 5 + b, 32 * b, min(32 * b + 32, PEERS - 1))

    whole(pack_b0, got_b0, 4).wait_recv()
    to_partner(got_b0, passed_b0, 9).start()
    widen(got_b0, wide_b0)
    y = 2 * lax.div(row, 8) + lax.div(col, 4)
    for b in range(4):
        y2 = lax.rem(y + 4 - ring(4, b), 4)
        base = 64 * lax.div(y2, 2) + 4 * lax.rem(y2, 2)
        whole(pack_b1, got_b1, 5 + b, 32 if b < 3 else 31).wait_recv()

        def pass_on(z, _):
            at = pl.multiple_of(2 * (base + 8 * z), 8)
            to_partner(got_b1.at[pl.ds(at, 8)], passed_b1.at[pl.ds(at, 8)], 10 + b).start()
            return 0

        def open_up(z, _):
            at = pl.multiple_of(2 * (base + 8 * z), 8)
            wide_b1[pl.ds(8 * at, 64), :] = got_b1[pl.ds(at, 8)].astype(F32).reshape(64, NR)
            return 0

        lax.fori_loop(0, 8, pass_on, 0)
        lax.fori_loop(0, 8, open_up, 0)

    order_sums(wide_b0, wide_b1, table_t, lambda t, value: sum_ref.__setitem__(t, value))

    to_partner(got_b0, passed_b0, 9).wait_recv()
    for b in range(4):
        to_partner(got_b1.at[pl.ds(0, 64)], passed_b1.at[pl.ds(0, 64)], 10 + b).wait_recv()
    for b in range(4):
        to_partner(got_b1.at[pl.ds(0, 64)], passed_b1.at[pl.ds(0, 64)], 10 + b).wait_send()
        whole(pack_b1, got_b1, 5 + b, 32 if b < 3 else 31).wait_send()
    to_partner(got_b0, passed_b0, 9).wait_send()
    whole(pack_b0, got_b0, 4).wait_send()
    whole(pack_a1, got_a1, 3).wait_send()
    whole(pack_a0, got_a0, 2).wait_send()
    to_partner(give_a1, taken_a1, 1).wait_send()
    to_partner(give_a0, taken_a0, 0).wait_send()


def back(wide_b0, wide_b1, c, parity, t):
    at = 12 * c + 6 * parity + t
    return (wide_b0, pl.ds(at, PEERS, stride=8)) if at < 8 else (wide_b1, pl.ds(at - 8, PEERS, stride=16))


def widen(got, wide):
    def body(i, _):
        wide[pl.ds(256 * i, 256), :] = got[pl.ds(32 * i, 32)].astype(F32).reshape(256, NR)
        return 0

    lax.fori_loop(0, got.shape[0] // 32, body, 0)


def order_sums(wide_b0, wide_b1, table, put):
    for k in range(LAT // 2):
        halves = []
        for t in (2 * k, 2 * k + 1):
            pieces = []
            for parity in range(2):
                for c in range(2):
                    wide, span = back(wide_b0, wide_b1, c, parity, t)
                    pieces.append(wide[span, :].astype(BF16))
            halves.append(jnp.concatenate(pieces, axis=0))
        sums = dot(table[...], jnp.concatenate(halves, axis=1))
        for j in range(2):
            put(2 * k + j, sums[:, j * NR : (j + 1) * NR])


def join(sum_ref, table_ref, passed_b0, passed_b1, new_ref, evolved_hbm, new_hbm, total, wide_b0, wide_b1, sem):
    copies = [pltpu.make_async_copy(new_ref, new_hbm, sem.at[LAT])]
    copies[0].start()
    widen(passed_b0, wide_b0)
    widen(passed_b1, wide_b1)

    def put(t, value):
        total[t] = sum_ref[t] + value
        copies.append(pltpu.make_async_copy(total.at[t], evolved_hbm.at[t], sem.at[t]))
        copies[-1].start()

    order_sums(wide_b0, wide_b1, table_ref, put)
    for copy in copies:
        copy.wait()


def on_device(grid_terms, pair_orders, legendre, state, kappa, right_op, left_op):
    vmem = pl.BlockSpec(memory_space=pltpu.VMEM)
    hbm = pl.BlockSpec(memory_space=pltpu.HBM)
    mib = 1024 * 1024
    grid_shape = (LAT, HALF, NR)
    spectral_shape = (1, DEG + 1, 2 * NR)

    def tiles_of(count):
        return (count * PEERS, 8, NR)

    parts = pl.pallas_call(
        kernel,
        out_shape=(
            jax.ShapeDtypeStruct(grid_shape, F32),
            jax.ShapeDtypeStruct((HALF, 4 * PEERS), BF16),
            jax.ShapeDtypeStruct(tiles_of(1), BF16),
            jax.ShapeDtypeStruct(tiles_of(2), BF16),
            jax.ShapeDtypeStruct(spectral_shape, BF16),
        ),
        in_specs=[hbm] * 7,
        out_specs=(vmem,) * 5,
        scratch_shapes=[
            pltpu.SMEM((2, PEERS), jnp.int32),
            pltpu.VMEM((2, PEERS), jnp.int32),
            pltpu.VMEM((1, NR), F32),
            pltpu.VMEM((NR, NR), BF16),
            pltpu.VMEM((NR, NR), BF16),
            pltpu.VMEM(grid_shape, F32),
            pltpu.VMEM(grid_shape, BF16),
            pltpu.VMEM((2, 4 * PEERS, HALF), BF16),
            pltpu.VMEM((HALF, 4 * PEERS), BF16),
        ]
        + [pltpu.VMEM((count * 8 * PEERS, NR), F32) for count in (2, 1, 1, 2)]
        + [pltpu.VMEM(tiles_of(count), BF16) for count in (2, 1, 1, 2, 2, 1, 1, 2, 2, 1, 2, 1)]
        + [
            pltpu.VMEM((DEG + 1, NTH), BF16),
            pltpu.VMEM((NTH, NTH), BF16),
            pltpu.VMEM((DEG + 1, NTH), BF16),
            pltpu.VMEM((NTH, DEG), BF16),
            pltpu.VMEM((DEG + 1, 2 * NR), BF16),
            pltpu.VMEM((NTH, 2 * NR), BF16),
            pltpu.VMEM((DEG + 1, NR), F32),
            pltpu.SemaphoreType.DMA((LAT + 7,)),
            pltpu.SemaphoreType.DMA((14,)),
            pltpu.SemaphoreType.DMA((14,)),
        ],
        compiler_params=pltpu.CompilerParams(collective_id=0, has_side_effects=True, vmem_limit_bytes=36 * mib),
    )(
        *(
            pltpu.with_memory_space_constraint(array, pltpu.HBM)
            for array in (
                pair_orders.reshape(2, PEERS), kappa.reshape(1, NR), right_op, left_op, grid_terms, legendre, state,
            )
        )
    )
    return pl.pallas_call(
        join,
        out_shape=(jax.ShapeDtypeStruct(grid_shape, F32), jax.ShapeDtypeStruct(spectral_shape, BF16)),
        in_specs=[vmem] * 5,
        out_specs=(hbm, hbm),
        scratch_shapes=[
            pltpu.VMEM(grid_shape, F32),
            pltpu.VMEM((8 * PEERS, NR), F32),
            pltpu.VMEM((16 * PEERS, NR), F32),
            pltpu.SemaphoreType.DMA((LAT + 1,)),
        ],
        compiler_params=pltpu.CompilerParams(vmem_limit_bytes=16 * mib),
    )(*parts)


def solution(mesh):
    return jax.shard_map(
        on_device,
        mesh=mesh,
        in_specs=(
            P(("row", "col"), "sec", None),
            P(),
            P(("sec", "row", "col"), None, None),
            P(("sec", "row", "col"), None, None),
            P(),
            P(),
            P(),
        ),
        out_specs=(P(("row", "col"), "sec", None), P(("sec", "row", "col"), None, None)),
        check_vma=False,
    )
```

```python
import functools
import math

import jax
import jax.numpy as jnp
from jax import lax
from jax.experimental import pallas as pl
from jax.experimental.pallas import tpu as pltpu
from jax.sharding import PartitionSpec as P

time_step = 0.5
filter_strength = 36.0
MESH = pl.DeviceIdType.MESH
F32 = jnp.float32
BF16 = jnp.bfloat16

LAT = 6
HALF = 768
NR = 128
PEERS = 128
DEG = 512
NTH = 768


GIVE_A0, GIVE_A1, TO_A0, TO_A1, TO_B0, TO_B1, PASS_B0, PASS_B1, SEMS = 0, 4, 5, 6, 7, 8, 12, 13, 17


def ring(count, k):
    return count // 2 + lax.div(k + 1, 2) * (1 - 2 * lax.rem(k, 2))


def peer_of(i, row, col):
    z, y, x = lax.rem(row, 8), 2 * lax.div(row, 8) + lax.div(col, 4), lax.rem(col, 4)
    z2 = lax.rem(z + ring(8, lax.rem(i, 8)), 8)
    x2 = lax.rem(x + ring(4, lax.rem(lax.div(i, 8), 4)), 4)
    y2 = lax.rem(y + ring(4, lax.div(i, 32)), 4)
    return 8 * lax.div(y2, 2) + z2, 4 * lax.rem(y2, 2) + x2


def wave(order, longitude):
    longitudes = 2 * HALF
    phase = order * longitude
    turns = jnp.round(phase * (1.0 / longitudes))
    angle = (phase - turns * longitudes) * (math.pi / longitudes)
    square = angle * angle
    sine = angle * (1.0 + square * (-1 / 6 + square * (1 / 120 + square * (-1 / 5040 + square * (1 / 362880)))))
    cosine = 1.0 + square * (
        -1 / 2 + square * (1 / 24 + square * (-1 / 720 + square * (1 / 40320 - square * (1 / 3628800))))
    )
    scale = 1.0 / math.sqrt(longitudes)
    return scale - (2.0 * scale) * sine * sine, (-2.0 * scale) * sine * cosine


def dot(a, b):
    return jnp.dot(a, b, preferred_element_type=F32)


def kernel(
    orders_hbm, kappa_hbm, right_hbm, left_hbm, grid_hbm, legendre_hbm, state_hbm,
    sum_ref, table_other, other_b0, other_b1, new_ref,
    orders_s, orders_v, kappa, right, left,
    grid, grid_low, table, table_t,
    wide_a0, wide_a1, wide_b0, wide_b1, pack_a0, pack_a1, pack_b0, pack_b1, got_a0, got_a1, got_b0, got_b1,
    give_a0, give_a1, taken_a0, taken_a1, passed_b0, passed_b1,
    legendre, permute, rows, rows_t, state, columns, factor,
    load_sem, send_sem, recv_sem,
):
    sec, row, col = lax.axis_index("sec"), lax.axis_index("row"), lax.axis_index("col")
    me = 8 * row + col
    partner = (1 - sec, row, col)
    sign = (1 - 2 * sec).astype(F32)

    loads = [pltpu.make_async_copy(orders_hbm, orders_v, load_sem.at[0])]
    loads += [pltpu.make_async_copy(grid_hbm.at[t], grid.at[t], load_sem.at[t + 1]) for t in range(LAT)]
    for source, target in (
        (orders_hbm, orders_s), (legendre_hbm.at[0], legendre), (state_hbm.at[0], state),
        (kappa_hbm, kappa), (right_hbm, right), (left_hbm, left),
    ):
        loads.append(pltpu.make_async_copy(source, target, load_sem.at[len(loads)]))
    for load in loads:
        load.start()

    barrier = pltpu.get_barrier_semaphore()

    def greet(i, _):
        row2, col2 = peer_of(i, row, col)
        pl.semaphore_signal(barrier, inc=1, device_id=(sec, row2, col2), device_id_type=MESH)
        return 0

    pl.semaphore_signal(barrier, inc=1, device_id=partner, device_id_type=MESH)
    lax.fori_loop(0, PEERS - 1, greet, 0)

    loads[0].wait()
    evens = []
    for which in range(2):
        low = orders_v[pl.ds(sec if which == 0 else 1 - sec, 1), :]
        evens.append(jnp.where(lax.rem(low, 2) == 0, low, DEG - 1 - low).astype(F32))

    for which in range(2):
        even_t = jnp.transpose(jnp.broadcast_to(evens[which], (PEERS, PEERS)))
        real, imag = wave(even_t, lax.broadcasted_iota(jnp.int32, (PEERS, 128), 1).astype(F32))
        turn_real, turn_imag = wave(even_t, 128.0)
        turn_real, turn_imag = turn_real * math.sqrt(2 * HALF), turn_imag * math.sqrt(2 * HALF)
        for lane in range(HALF // 128):
            longitude = (lax.broadcasted_iota(jnp.int32, (8, 128), 1) + 128 * lane).astype(F32)
            last_real, last_imag = wave(jnp.full((8, 128), DEG - 1.0, F32), longitude)
            last_real = (last_real * (sign * math.sqrt(2 * HALF)))[:1]
            last_imag = (last_imag * (sign * math.sqrt(2 * HALF)))[:1]
            span = pl.ds(128 * lane, 128)
            table[which, 0:PEERS, span] = real.astype(BF16)
            table[which, PEERS : 2 * PEERS, span] = imag.astype(BF16)
            table[which, 2 * PEERS : 3 * PEERS, span] = (last_real * real + last_imag * imag).astype(BF16)
            table[which, 3 * PEERS :, span] = (last_imag * real - last_real * imag).astype(BF16)
            real, imag = real * turn_real - imag * turn_imag, imag * turn_real + real * turn_imag

    def there(c, parity, t):
        at = 12 * c + 6 * parity + t
        return (wide_a0, pl.ds(at, PEERS, stride=16)) if at < 16 else (wide_a1, pl.ds(at - 16, PEERS, stride=8))

    def narrow(wide, pack, added=None):
        def body(i, _):
            values = wide[pl.ds(256 * i, 256), :].reshape(32, 8, NR)
            if added is not None:
                values = values + added[pl.ds(32 * i, 32)].astype(F32)
            pack[pl.ds(32 * i, 32)] = values.astype(BF16)
            return 0

        lax.fori_loop(0, pack.shape[0] // 32, body, 0)

    for t in range(LAT):
        loads[t + 1].wait()
        grid_low[t] = grid[t].astype(BF16)
    for which in (1, 0):
        for k in range(LAT // 2):
            values = jnp.concatenate([grid_low[2 * k], grid_low[2 * k + 1]], axis=1)
            sums = dot(table[which], values)
            for parity in range(2):
                for c in range(2):
                    for j in range(2):
                        wide, span = there(c, parity, 2 * k + j)
                        at = (2 * parity + c) * PEERS
                        wide[span, :] = sums[at : at + PEERS, j * NR : (j + 1) * NR]
        if which == 1:
            narrow(wide_a0, give_a0)
            narrow(wide_a1, give_a1)

    pl.semaphore_wait(barrier, PEERS)

    def to_partner(source, target, sem):
        return pltpu.make_async_remote_copy(
            source, target, send_sem.at[sem], recv_sem.at[sem], device_id=partner, device_id_type=MESH
        )

    y = 2 * lax.div(row, 8) + lax.div(col, 4)

    def run_of(y2, z):
        return pl.multiple_of(2 * (64 * lax.div(y2, 2) + 4 * lax.rem(y2, 2) + 8 * z), 8)

    def runs(body):
        def step(z, _):
            body(z)
            return 0

        lax.fori_loop(0, 8, step, 0)

    def send_runs(source, target, y2, sem):
        def body(z):
            at = run_of(y2, z)
            to_partner(source.at[pl.ds(at, 8)], target.at[pl.ds(at, 8)], sem).start()

        runs(body)

    def sent_runs(source, target, sem):
        return to_partner(source.at[pl.ds(0, 64)], target.at[pl.ds(0, 64)], sem)

    def widen_runs(got, wide, y2):
        def body(z):
            at = run_of(y2, z)
            wide[pl.ds(8 * at, 64), :] = got[pl.ds(at, 8)].astype(F32).reshape(64, NR)

        runs(body)

    for b in range(4):
        send_runs(give_a0, taken_a0, lax.rem(y + ring(4, b), 4), GIVE_A0 + b)
    to_partner(give_a1, taken_a1, GIVE_A1).start()

    def exchange(pack, got, sem, start=0, stop=PEERS - 1):
        tiles = pack.shape[0] // PEERS

        def body(i, _):
            row2, col2 = peer_of(i, row, col)
            pltpu.make_async_remote_copy(
                pack.at[pl.ds(tiles * (8 * row2 + col2), tiles)], got.at[pl.ds(tiles * me, tiles)],
                send_sem.at[sem], recv_sem.at[sem], device_id=(sec, row2, col2), device_id_type=MESH,
            ).start()
            return 0

        lax.fori_loop(start, stop, body, 0)
        if stop == PEERS - 1:
            got[pl.ds(tiles * me, tiles)] = pack[pl.ds(tiles * me, tiles)]

    def whole(pack, got, sem, messages=PEERS - 1):
        count = pack.shape[0] // PEERS * messages
        return to_partner(pack.at[pl.ds(0, count)], got.at[pl.ds(0, count)], sem)

    for b in range(4):
        sent_runs(give_a0, taken_a0, GIVE_A0 + b).wait_recv()

        def add(z):
            at = run_of(lax.rem(y + ring(4, b), 4), z)
            values = wide_a0[pl.ds(8 * at, 64), :].reshape(8, 8, NR) + taken_a0[pl.ds(at, 8)].astype(F32)
            pack_a0[pl.ds(at, 8)] = values.astype(BF16)

        runs(add)
        exchange(pack_a0, got_a0, TO_A0, 32 * b, min(32 * b + 32, PEERS - 1))
    to_partner(give_a1, taken_a1, GIVE_A1).wait_recv()
    narrow(wide_a1, pack_a1, taken_a1)
    exchange(pack_a1, got_a1, TO_A1)

    for load in loads[LAT + 1 :]:
        load.wait()
    for lane in range(HALF // 128):
        longitude = (lax.broadcasted_iota(jnp.int32, (128, PEERS), 0) + 128 * lane).astype(F32)
        span = pl.ds(128 * lane, 128)
        for which in range(2):
            for parity in range(2):
                order = evens[which] if parity == 0 else (DEG - 1.0) - evens[which]
                real, imag = wave(jnp.broadcast_to(order, (128, PEERS)), longitude)
                if parity == 1:
                    real, imag = real * sign, imag * sign
                target = table_t if which == 0 else table_other
                at = 2 * PEERS * parity
                target[span, at : at + PEERS] = real.astype(BF16)
                target[span, at + PEERS : at + 2 * PEERS] = imag.astype(BF16)
    for t in range(LAT):
        latitude = lax.broadcasted_iota(jnp.int32, (NTH, PEERS), 0)
        device = lax.broadcasted_iota(jnp.int32, (NTH, PEERS), 1)
        permute[:, t * PEERS : (t + 1) * PEERS] = jnp.where(latitude == LAT * device + t, 1.0, 0.0).astype(BF16)
    rows[...] = dot(legendre[...], permute[...]).astype(BF16)
    for i in range(4):
        for j in range(LAT):
            rows_t[pl.ds(128 * j, 128), pl.ds(128 * i, 128)] = jnp.transpose(
                rows[pl.ds(128 * i, 128), pl.ds(128 * j, 128)].astype(F32)
            ).astype(BF16)
    mine = orders_s[sec, me]
    index = lax.broadcasted_iota(jnp.int32, (DEG + 1, NR), 0)
    leading = index < DEG - mine
    first = leading == (lax.rem(mine, 2) == 0)
    degree = jnp.where(leading, mine + index, index - 1).astype(F32)
    mode = lax.broadcasted_iota(jnp.int32, (1, NR), 1).astype(F32) * (1.0 / NR)
    mode4 = (mode * mode) * (mode * mode)
    mode8 = mode4 * mode4
    mode16 = mode8 * mode8
    damping = jnp.exp(-filter_strength * (mode16 * mode16 * mode4))
    factor[...] = damping / (1.0 + kappa[...] + degree * (degree + 1.0) * (1.0 / (DEG * DEG)))

    for c in range(2):
        if c == 0:
            whole(pack_a0, got_a0, TO_A0).wait_recv()
            widen(got_a0, wide_a0)
        else:
            whole(pack_a1, got_a1, TO_A1).wait_recv()
            widen(got_a1, wide_a1)
        for parity in range(2):
            for t in range(LAT):
                wide, span = there(c, parity, t)
                columns[t * PEERS : (t + 1) * PEERS, parity * NR : (parity + 1) * NR] = wide[span, :].astype(BF16)
        both = dot(rows[...], columns[...])
        coefficient = jnp.where(first, both[:, :NR], both[:, NR:])
        right_side = state[:, c * NR : (c + 1) * NR].astype(F32) + time_step * coefficient
        scaled = (dot(right_side.astype(BF16), right[...]) * factor[...]).astype(BF16)
        new = dot(scaled, left[...]).astype(BF16)
        new_ref[0, :, c * NR : (c + 1) * NR] = new
        new = new.astype(F32)
        split = jnp.concatenate([jnp.where(first, new, 0.0), jnp.where(first, 0.0, new)], axis=1)
        tail = split[DEG:, :]
        ends = jnp.transpose(jnp.broadcast_to(rows[DEG:, :].astype(F32), (128, NTH)))
        ends = jnp.concatenate([ends, ends], axis=1)
        sums = dot(rows_t[...], split[:DEG, :].astype(BF16)) + ends * tail
        for parity in range(2):
            for t in range(LAT):
                wide, span = back(wide_b0, wide_b1, c, parity, t)
                wide[span, :] = sums[t * PEERS : (t + 1) * PEERS, parity * NR : (parity + 1) * NR]
        if c == 0:
            narrow(wide_b0, pack_b0)
            exchange(pack_b0, got_b0, TO_B0)
        else:
            narrow(wide_b1, pack_b1)
            for b in range(4):
                exchange(pack_b1, got_b1, TO_B1 + b, 32 * b, min(32 * b + 32, PEERS - 1))

    whole(pack_b0, got_b0, TO_B0).wait_recv()
    to_partner(got_b0, passed_b0, PASS_B0).start()
    widen(got_b0, wide_b0)
    for b in range(4):
        y2 = lax.rem(y + 4 - ring(4, b), 4)
        whole(pack_b1, got_b1, TO_B1 + b, 32 if b < 3 else 31).wait_recv()
        send_runs(got_b1, passed_b1, y2, PASS_B1 + b)
        widen_runs(got_b1, wide_b1, y2)
        if b == 0:
            to_partner(got_b0, passed_b0, PASS_B0).wait_recv()
            widen(passed_b0, other_b0)
        else:
            sent_runs(got_b1, passed_b1, PASS_B1 + b - 1).wait_recv()
            widen_runs(passed_b1, other_b1, lax.rem(y + 4 - ring(4, b - 1), 4))

    order_sums(wide_b0, wide_b1, table_t, lambda t, value: sum_ref.__setitem__(t, value))

    sent_runs(got_b1, passed_b1, PASS_B1 + 3).wait_recv()
    widen_runs(passed_b1, other_b1, y)
    for b in range(4):
        sent_runs(got_b1, passed_b1, PASS_B1 + b).wait_send()
        whole(pack_b1, got_b1, TO_B1 + b, 32 if b < 3 else 31).wait_send()
        sent_runs(give_a0, taken_a0, GIVE_A0 + b).wait_send()
    to_partner(got_b0, passed_b0, PASS_B0).wait_send()
    whole(pack_b0, got_b0, TO_B0).wait_send()
    whole(pack_a1, got_a1, TO_A1).wait_send()
    whole(pack_a0, got_a0, TO_A0).wait_send()
    to_partner(give_a1, taken_a1, GIVE_A1).wait_send()


def back(wide_b0, wide_b1, c, parity, t):
    at = 12 * c + 6 * parity + t
    return (wide_b0, pl.ds(at, PEERS, stride=8)) if at < 8 else (wide_b1, pl.ds(at - 8, PEERS, stride=16))


def widen(got, wide):
    def body(i, _):
        wide[pl.ds(256 * i, 256), :] = got[pl.ds(32 * i, 32)].astype(F32).reshape(256, NR)
        return 0

    lax.fori_loop(0, got.shape[0] // 32, body, 0)


def order_sums(wide_b0, wide_b1, table, put):
    for k in range(LAT // 2):
        halves = []
        for t in (2 * k, 2 * k + 1):
            pieces = []
            for parity in range(2):
                for c in range(2):
                    wide, span = back(wide_b0, wide_b1, c, parity, t)
                    pieces.append(wide[span, :].astype(BF16))
            halves.append(jnp.concatenate(pieces, axis=0))
        sums = dot(table[...], jnp.concatenate(halves, axis=1))
        for j in range(2):
            put(2 * k + j, sums[:, j * NR : (j + 1) * NR])


def join(sum_ref, table_ref, wide_b0, wide_b1, new_ref, evolved_hbm, new_hbm, total, sem):
    copies = [pltpu.make_async_copy(new_ref, new_hbm, sem.at[LAT])]
    copies[0].start()

    def put(t, value):
        total[t] = sum_ref[t] + value
        copies.append(pltpu.make_async_copy(total.at[t], evolved_hbm.at[t], sem.at[t]))
        copies[-1].start()

    order_sums(wide_b0, wide_b1, table_ref, put)
    for copy in copies:
        copy.wait()


def on_device(grid_terms, pair_orders, legendre, state, kappa, right_op, left_op):
    vmem = pl.BlockSpec(memory_space=pltpu.VMEM)
    hbm = pl.BlockSpec(memory_space=pltpu.HBM)
    mib = 1024 * 1024
    grid_shape = (LAT, HALF, NR)
    spectral_shape = (1, DEG + 1, 2 * NR)

    def tiles_of(count):
        return (count * PEERS, 8, NR)

    parts = pl.pallas_call(
        kernel,
        out_shape=(
            jax.ShapeDtypeStruct(grid_shape, F32),
            jax.ShapeDtypeStruct((HALF, 4 * PEERS), BF16),
            jax.ShapeDtypeStruct((8 * PEERS, NR), F32),
            jax.ShapeDtypeStruct((16 * PEERS, NR), F32),
            jax.ShapeDtypeStruct(spectral_shape, BF16),
        ),
        in_specs=[hbm] * 7,
        out_specs=(vmem,) * 5,
        scratch_shapes=[
            pltpu.SMEM((2, PEERS), jnp.int32),
            pltpu.VMEM((2, PEERS), jnp.int32),
            pltpu.VMEM((1, NR), F32),
            pltpu.VMEM((NR, NR), BF16),
            pltpu.VMEM((NR, NR), BF16),
            pltpu.VMEM(grid_shape, F32),
            pltpu.VMEM(grid_shape, BF16),
            pltpu.VMEM((2, 4 * PEERS, HALF), BF16),
            pltpu.VMEM((HALF, 4 * PEERS), BF16),
        ]
        + [pltpu.VMEM((count * 8 * PEERS, NR), F32) for count in (2, 1, 1, 2)]
        + [pltpu.VMEM(tiles_of(count), BF16) for count in (2, 1, 1, 2, 2, 1, 1, 2, 2, 1, 2, 1, 1, 2)]
        + [
            pltpu.VMEM((DEG + 1, NTH), BF16),
            pltpu.VMEM((NTH, NTH), BF16),
            pltpu.VMEM((DEG + 1, NTH), BF16),
            pltpu.VMEM((NTH, DEG), BF16),
            pltpu.VMEM((DEG + 1, 2 * NR), BF16),
            pltpu.VMEM((NTH, 2 * NR), BF16),
            pltpu.VMEM((DEG + 1, NR), F32),
            pltpu.SemaphoreType.DMA((LAT + 7,)),
            pltpu.SemaphoreType.DMA((SEMS,)),
            pltpu.SemaphoreType.DMA((SEMS,)),
        ],
        compiler_params=pltpu.CompilerParams(collective_id=0, has_side_effects=True, vmem_limit_bytes=36 * mib),
    )(
        *(
            pltpu.with_memory_space_constraint(array, pltpu.HBM)
            for array in (
                pair_orders.reshape(2, PEERS), kappa.reshape(1, NR), right_op, left_op, grid_terms, legendre, state,
            )
        )
    )
    return pl.pallas_call(
        join,
        out_shape=(jax.ShapeDtypeStruct(grid_shape, F32), jax.ShapeDtypeStruct(spectral_shape, BF16)),
        in_specs=[vmem] * 5,
        out_specs=(hbm, hbm),
        scratch_shapes=[
            pltpu.VMEM(grid_shape, F32),
            pltpu.SemaphoreType.DMA((LAT + 1,)),
        ],
        compiler_params=pltpu.CompilerParams(vmem_limit_bytes=16 * mib),
    )(*parts)


def solution(mesh):
    return jax.shard_map(
        on_device,
        mesh=mesh,
        in_specs=(
            P(("row", "col"), "sec", None),
            P(),
            P(("sec", "row", "col"), None, None),
            P(("sec", "row", "col"), None, None),
            P(),
            P(),
            P(),
        ),
        out_specs=(P(("row", "col"), "sec", None), P(("sec", "row", "col"), None, None)),
        check_vma=False,
    )
```

```python
import functools
import math

import jax
import jax.numpy as jnp
from jax import lax
from jax.experimental import pallas as pl
from jax.experimental.pallas import tpu as pltpu
from jax.sharding import PartitionSpec as P

time_step = 0.5
filter_strength = 36.0
MESH = pl.DeviceIdType.MESH
F32 = jnp.float32
BF16 = jnp.bfloat16

LAT = 6
HALF = 768
NR = 128
PEERS = 128
DEG = 512
NTH = 768


GIVE_A0, GIVE_A1, TO_A0, TO_A1, TO_B0, TO_B1, PASS_B0, PASS_B1, SEMS = 0, 4, 5, 6, 7, 8, 12, 13, 17


def ring(count, k):
    return count // 2 + (k + 1) // 2 * (1 - 2 * (k % 2))


def each_peer(row, col, body, first=0, last=16):
    z, y, x = lax.rem(row, 8), 2 * lax.div(row, 8) + lax.div(col, 4), lax.rem(col, 4)
    along = [lax.rem(z + ring(8, k), 8) for k in range(8)]

    def line(i, count):
        x2 = lax.rem(x + ring(4, lax.rem(i, 4)), 4)
        y2 = lax.rem(y + ring(4, lax.div(i, 4)), 4)
        row2, col2 = 8 * lax.div(y2, 2), 4 * lax.rem(y2, 2) + x2
        for z2 in along[:count]:
            body(row2 + z2, col2)

    def step(i, _):
        line(i, 8)
        return 0

    lax.fori_loop(first, min(last, 15), step, 0)
    if last == 16:
        line(jnp.int32(15), 7)


def wave(order, longitude):
    longitudes = 2 * HALF
    phase = order * longitude
    turns = jnp.round(phase * (1.0 / longitudes))
    angle = (phase - turns * longitudes) * (math.pi / longitudes)
    square = angle * angle
    sine = angle * (1.0 + square * (-1 / 6 + square * (1 / 120 + square * (-1 / 5040 + square * (1 / 362880)))))
    cosine = 1.0 + square * (
        -1 / 2 + square * (1 / 24 + square * (-1 / 720 + square * (1 / 40320 - square * (1 / 3628800))))
    )
    scale = 1.0 / math.sqrt(longitudes)
    return scale - (2.0 * scale) * sine * sine, (-2.0 * scale) * sine * cosine


def dot(a, b):
    return jnp.dot(a, b, preferred_element_type=F32)


def kernel(
    orders_hbm, kappa_hbm, right_hbm, left_hbm, grid_hbm, legendre_hbm, state_hbm,
    sum_ref, table_other, other_b0, other_b1, new_ref,
    orders_s, orders_v, kappa, right, left,
    grid, grid_low, table, table_t,
    wide_a0, wide_a1, wide_b0, wide_b1, pack_a0, pack_a1, pack_b0, pack_b1, got_a0, got_a1, got_b0, got_b1,
    give_a0, give_a1, taken_a0, taken_a1, passed_b0, passed_b1,
    legendre, permute, rows, rows_t, state, columns, factor,
    load_sem, send_sem, recv_sem,
):
    sec, row, col = lax.axis_index("sec"), lax.axis_index("row"), lax.axis_index("col")
    me = 8 * row + col
    partner = (1 - sec, row, col)
    sign = (1 - 2 * sec).astype(F32)

    loads = [pltpu.make_async_copy(orders_hbm, orders_v, load_sem.at[0])]
    loads += [pltpu.make_async_copy(grid_hbm.at[t], grid.at[t], load_sem.at[t + 1]) for t in range(LAT)]
    for source, target in (
        (orders_hbm, orders_s), (legendre_hbm.at[0], legendre), (state_hbm.at[0], state),
        (kappa_hbm, kappa), (right_hbm, right), (left_hbm, left),
    ):
        loads.append(pltpu.make_async_copy(source, target, load_sem.at[len(loads)]))
    for load in loads:
        load.start()

    barrier = pltpu.get_barrier_semaphore()

    def greet(row2, col2):
        pl.semaphore_signal(barrier, inc=1, device_id=(sec, row2, col2), device_id_type=MESH)

    pl.semaphore_signal(barrier, inc=1, device_id=partner, device_id_type=MESH)
    each_peer(row, col, greet)

    loads[0].wait()
    evens = []
    for which in range(2):
        low = orders_v[pl.ds(sec if which == 0 else 1 - sec, 1), :]
        evens.append(jnp.where(lax.rem(low, 2) == 0, low, DEG - 1 - low).astype(F32))

    for which in range(2):
        even_t = jnp.transpose(jnp.broadcast_to(evens[which], (PEERS, PEERS)))
        real, imag = wave(even_t, lax.broadcasted_iota(jnp.int32, (PEERS, 128), 1).astype(F32))
        turn_real, turn_imag = wave(even_t, 128.0)
        turn_real, turn_imag = turn_real * math.sqrt(2 * HALF), turn_imag * math.sqrt(2 * HALF)
        for lane in range(HALF // 128):
            longitude = (lax.broadcasted_iota(jnp.int32, (8, 128), 1) + 128 * lane).astype(F32)
            last_real, last_imag = wave(jnp.full((8, 128), DEG - 1.0, F32), longitude)
            last_real = (last_real * (sign * math.sqrt(2 * HALF)))[:1]
            last_imag = (last_imag * (sign * math.sqrt(2 * HALF)))[:1]
            span = pl.ds(128 * lane, 128)
            table[which, 0:PEERS, span] = real.astype(BF16)
            table[which, PEERS : 2 * PEERS, span] = imag.astype(BF16)
            table[which, 2 * PEERS : 3 * PEERS, span] = (last_real * real + last_imag * imag).astype(BF16)
            table[which, 3 * PEERS :, span] = (last_imag * real - last_real * imag).astype(BF16)
            real, imag = real * turn_real - imag * turn_imag, imag * turn_real + real * turn_imag

    def there(c, parity, t):
        at = 12 * c + 6 * parity + t
        return (wide_a0, pl.ds(at, PEERS, stride=16)) if at < 16 else (wide_a1, pl.ds(at - 16, PEERS, stride=8))

    def narrow(wide, pack, added=None):
        def body(i, _):
            values = wide[pl.ds(256 * i, 256), :].reshape(32, 8, NR)
            if added is not None:
                values = values + added[pl.ds(32 * i, 32)].astype(F32)
            pack[pl.ds(32 * i, 32)] = values.astype(BF16)
            return 0

        lax.fori_loop(0, pack.shape[0] // 32, body, 0)

    for t in range(LAT):
        loads[t + 1].wait()
        grid_low[t] = grid[t].astype(BF16)
    for which in (1, 0):
        for k in range(LAT // 2):
            values = jnp.concatenate([grid_low[2 * k], grid_low[2 * k + 1]], axis=1)
            sums = dot(table[which], values)
            for parity in range(2):
                for c in range(2):
                    for j in range(2):
                        wide, span = there(c, parity, 2 * k + j)
                        at = (2 * parity + c) * PEERS
                        wide[span, :] = sums[at : at + PEERS, j * NR : (j + 1) * NR]
        if which == 1:
            narrow(wide_a0, give_a0)
            narrow(wide_a1, give_a1)

    pl.semaphore_wait(barrier, PEERS)

    def to_partner(source, target, sem):
        return pltpu.make_async_remote_copy(
            source, target, send_sem.at[sem], recv_sem.at[sem], device_id=partner, device_id_type=MESH
        )

    y = 2 * lax.div(row, 8) + lax.div(col, 4)

    def run_of(y2, z):
        return pl.multiple_of(2 * (64 * lax.div(y2, 2) + 4 * lax.rem(y2, 2) + 8 * z), 8)

    def runs(body):
        def step(z, _):
            body(z)
            return 0

        lax.fori_loop(0, 8, step, 0)

    def send_runs(source, target, y2, sem):
        def body(z):
            at = run_of(y2, z)
            to_partner(source.at[pl.ds(at, 8)], target.at[pl.ds(at, 8)], sem).start()

        runs(body)

    def sent_runs(source, target, sem):
        return to_partner(source.at[pl.ds(0, 64)], target.at[pl.ds(0, 64)], sem)

    def widen_runs(got, wide, y2):
        def body(z):
            at = run_of(y2, z)
            wide[pl.ds(8 * at, 64), :] = got[pl.ds(at, 8)].astype(F32).reshape(64, NR)

        runs(body)

    for b in range(4):
        send_runs(give_a0, taken_a0, lax.rem(y + ring(4, b), 4), GIVE_A0 + b)
    to_partner(give_a1, taken_a1, GIVE_A1).start()

    def exchange(pack, got, sem, first=0, last=16):
        tiles = pack.shape[0] // PEERS

        def send(row2, col2):
            pltpu.make_async_remote_copy(
                pack.at[pl.ds(tiles * (8 * row2 + col2), tiles)], got.at[pl.ds(tiles * me, tiles)],
                send_sem.at[sem], recv_sem.at[sem], device_id=(sec, row2, col2), device_id_type=MESH,
            ).start()

        each_peer(row, col, send, first, last)
        if last == 16:
            got[pl.ds(tiles * me, tiles)] = pack[pl.ds(tiles * me, tiles)]

    def whole(pack, got, sem, messages=PEERS - 1):
        count = pack.shape[0] // PEERS * messages
        return to_partner(pack.at[pl.ds(0, count)], got.at[pl.ds(0, count)], sem)

    for b in range(4):
        sent_runs(give_a0, taken_a0, GIVE_A0 + b).wait_recv()

        def add(z):
            at = run_of(lax.rem(y + ring(4, b), 4), z)
            values = wide_a0[pl.ds(8 * at, 64), :].reshape(8, 8, NR) + taken_a0[pl.ds(at, 8)].astype(F32)
            pack_a0[pl.ds(at, 8)] = values.astype(BF16)

        runs(add)
        exchange(pack_a0, got_a0, TO_A0, 4 * b, 4 * b + 4)
    to_partner(give_a1, taken_a1, GIVE_A1).wait_recv()
    narrow(wide_a1, pack_a1, taken_a1)
    exchange(pack_a1, got_a1, TO_A1)

    for load in loads[LAT + 1 :]:
        load.wait()
    for lane in range(HALF // 128):
        longitude = (lax.broadcasted_iota(jnp.int32, (128, PEERS), 0) + 128 * lane).astype(F32)
        span = pl.ds(128 * lane, 128)
        for which in range(2):
            for parity in range(2):
                order = evens[which] if parity == 0 else (DEG - 1.0) - evens[which]
                real, imag = wave(jnp.broadcast_to(order, (128, PEERS)), longitude)
                if parity == 1:
                    real, imag = real * sign, imag * sign
                target = table_t if which == 0 else table_other
                at = 2 * PEERS * parity
                target[span, at : at + PEERS] = real.astype(BF16)
                target[span, at + PEERS : at + 2 * PEERS] = imag.astype(BF16)
    for t in range(LAT):
        latitude = lax.broadcasted_iota(jnp.int32, (NTH, PEERS), 0)
        device = lax.broadcasted_iota(jnp.int32, (NTH, PEERS), 1)
        permute[:, t * PEERS : (t + 1) * PEERS] = jnp.where(latitude == LAT * device + t, 1.0, 0.0).astype(BF16)
    rows[...] = dot(legendre[...], permute[...]).astype(BF16)
    for i in range(4):
        for j in range(LAT):
            rows_t[pl.ds(128 * j, 128), pl.ds(128 * i, 128)] = jnp.transpose(
                rows[pl.ds(128 * i, 128), pl.ds(128 * j, 128)].astype(F32)
            ).astype(BF16)
    mine = orders_s[sec, me]
    index = lax.broadcasted_iota(jnp.int32, (DEG + 1, NR), 0)
    leading = index < DEG - mine
    first = leading == (lax.rem(mine, 2) == 0)
    degree = jnp.where(leading, mine + index, index - 1).astype(F32)
    mode = lax.broadcasted_iota(jnp.int32, (1, NR), 1).astype(F32) * (1.0 / NR)
    mode4 = (mode * mode) * (mode * mode)
    mode8 = mode4 * mode4
    mode16 = mode8 * mode8
    damping = jnp.exp(-filter_strength * (mode16 * mode16 * mode4))
    factor[...] = damping / (1.0 + kappa[...] + degree * (degree + 1.0) * (1.0 / (DEG * DEG)))

    for c in range(2):
        if c == 0:
            whole(pack_a0, got_a0, TO_A0).wait_recv()
            widen(got_a0, wide_a0)
        else:
            whole(pack_a1, got_a1, TO_A1).wait_recv()
            widen(got_a1, wide_a1)
        for parity in range(2):
            for t in range(LAT):
                wide, span = there(c, parity, t)
                columns[t * PEERS : (t + 1) * PEERS, parity * NR : (parity + 1) * NR] = wide[span, :].astype(BF16)
        both = dot(rows[...], columns[...])
        coefficient = jnp.where(first, both[:, :NR], both[:, NR:])
        right_side = state[:, c * NR : (c + 1) * NR].astype(F32) + time_step * coefficient
        scaled = (dot(right_side.astype(BF16), right[...]) * factor[...]).astype(BF16)
        new = dot(scaled, left[...]).astype(BF16)
        new_ref[0, :, c * NR : (c + 1) * NR] = new
        new = new.astype(F32)
        split = jnp.concatenate([jnp.where(first, new, 0.0), jnp.where(first, 0.0, new)], axis=1)
        tail = split[DEG:, :]
        ends = jnp.transpose(jnp.broadcast_to(rows[DEG:, :].astype(F32), (128, NTH)))
        ends = jnp.concatenate([ends, ends], axis=1)
        sums = dot(rows_t[...], split[:DEG, :].astype(BF16)) + ends * tail
        for parity in range(2):
            for t in range(LAT):
                wide, span = back(wide_b0, wide_b1, c, parity, t)
                wide[span, :] = sums[t * PEERS : (t + 1) * PEERS, parity * NR : (parity + 1) * NR]
        if c == 0:
            narrow(wide_b0, pack_b0)
            exchange(pack_b0, got_b0, TO_B0)
        else:
            narrow(wide_b1, pack_b1)
            for b in range(4):
                exchange(pack_b1, got_b1, TO_B1 + b, 4 * b, 4 * b + 4)

    whole(pack_b0, got_b0, TO_B0).wait_recv()
    to_partner(got_b0, passed_b0, PASS_B0).start()
    widen(got_b0, wide_b0)
    for b in range(4):
        y2 = lax.rem(y + 4 - ring(4, b), 4)
        whole(pack_b1, got_b1, TO_B1 + b, 32 if b < 3 else 31).wait_recv()
        send_runs(got_b1, passed_b1, y2, PASS_B1 + b)
        widen_runs(got_b1, wide_b1, y2)
        if b == 0:
            to_partner(got_b0, passed_b0, PASS_B0).wait_recv()
            widen(passed_b0, other_b0)
        else:
            sent_runs(got_b1, passed_b1, PASS_B1 + b - 1).wait_recv()
            widen_runs(passed_b1, other_b1, lax.rem(y + 4 - ring(4, b - 1), 4))

    order_sums(wide_b0, wide_b1, table_t, lambda t, value: sum_ref.__setitem__(t, value))

    sent_runs(got_b1, passed_b1, PASS_B1 + 3).wait_recv()
    widen_runs(passed_b1, other_b1, y)
    for b in range(4):
        sent_runs(got_b1, passed_b1, PASS_B1 + b).wait_send()
        whole(pack_b1, got_b1, TO_B1 + b, 32 if b < 3 else 31).wait_send()
        sent_runs(give_a0, taken_a0, GIVE_A0 + b).wait_send()
    to_partner(got_b0, passed_b0, PASS_B0).wait_send()
    whole(pack_b0, got_b0, TO_B0).wait_send()
    whole(pack_a1, got_a1, TO_A1).wait_send()
    whole(pack_a0, got_a0, TO_A0).wait_send()
    to_partner(give_a1, taken_a1, GIVE_A1).wait_send()


def back(wide_b0, wide_b1, c, parity, t):
    at = 12 * c + 6 * parity + t
    return (wide_b0, pl.ds(at, PEERS, stride=8)) if at < 8 else (wide_b1, pl.ds(at - 8, PEERS, stride=16))


def widen(got, wide):
    def body(i, _):
        wide[pl.ds(256 * i, 256), :] = got[pl.ds(32 * i, 32)].astype(F32).reshape(256, NR)
        return 0

    lax.fori_loop(0, got.shape[0] // 32, body, 0)


def order_sums(wide_b0, wide_b1, table, put):
    for k in range(LAT // 2):
        halves = []
        for t in (2 * k, 2 * k + 1):
            pieces = []
            for parity in range(2):
                for c in range(2):
                    wide, span = back(wide_b0, wide_b1, c, parity, t)
                    pieces.append(wide[span, :].astype(BF16))
            halves.append(jnp.concatenate(pieces, axis=0))
        sums = dot(table[...], jnp.concatenate(halves, axis=1))
        for j in range(2):
            put(2 * k + j, sums[:, j * NR : (j + 1) * NR])


def join(sum_ref, table_ref, wide_b0, wide_b1, new_ref, evolved_hbm, new_hbm, total, sem):
    copies = [pltpu.make_async_copy(new_ref, new_hbm, sem.at[LAT])]
    copies[0].start()

    def put(t, value):
        total[t] = sum_ref[t] + value
        copies.append(pltpu.make_async_copy(total.at[t], evolved_hbm.at[t], sem.at[t]))
        copies[-1].start()

    order_sums(wide_b0, wide_b1, table_ref, put)
    for copy in copies:
        copy.wait()


def on_device(grid_terms, pair_orders, legendre, state, kappa, right_op, left_op):
    vmem = pl.BlockSpec(memory_space=pltpu.VMEM)
    hbm = pl.BlockSpec(memory_space=pltpu.HBM)
    mib = 1024 * 1024
    grid_shape = (LAT, HALF, NR)
    spectral_shape = (1, DEG + 1, 2 * NR)

    def tiles_of(count):
        return (count * PEERS, 8, NR)

    parts = pl.pallas_call(
        kernel,
        out_shape=(
            jax.ShapeDtypeStruct(grid_shape, F32),
            jax.ShapeDtypeStruct((HALF, 4 * PEERS), BF16),
            jax.ShapeDtypeStruct((8 * PEERS, NR), F32),
            jax.ShapeDtypeStruct((16 * PEERS, NR), F32),
            jax.ShapeDtypeStruct(spectral_shape, BF16),
        ),
        in_specs=[hbm] * 7,
        out_specs=(vmem,) * 5,
        scratch_shapes=[
            pltpu.SMEM((2, PEERS), jnp.int32),
            pltpu.VMEM((2, PEERS), jnp.int32),
            pltpu.VMEM((1, NR), F32),
            pltpu.VMEM((NR, NR), BF16),
            pltpu.VMEM((NR, NR), BF16),
            pltpu.VMEM(grid_shape, F32),
            pltpu.VMEM(grid_shape, BF16),
            pltpu.VMEM((2, 4 * PEERS, HALF), BF16),
            pltpu.VMEM((HALF, 4 * PEERS), BF16),
        ]
        + [pltpu.VMEM((count * 8 * PEERS, NR), F32) for count in (2, 1, 1, 2)]
        + [pltpu.VMEM(tiles_of(count), BF16) for count in (2, 1, 1, 2, 2, 1, 1, 2, 2, 1, 2, 1, 1, 2)]
        + [
            pltpu.VMEM((DEG + 1, NTH), BF16),
            pltpu.VMEM((NTH, NTH), BF16),
            pltpu.VMEM((DEG + 1, NTH), BF16),
            pltpu.VMEM((NTH, DEG), BF16),
            pltpu.VMEM((DEG + 1, 2 * NR), BF16),
            pltpu.VMEM((NTH, 2 * NR), BF16),
            pltpu.VMEM((DEG + 1, NR), F32),
            pltpu.SemaphoreType.DMA((LAT + 7,)),
            pltpu.SemaphoreType.DMA((SEMS,)),
            pltpu.SemaphoreType.DMA((SEMS,)),
        ],
        compiler_params=pltpu.CompilerParams(collective_id=0, has_side_effects=True, vmem_limit_bytes=36 * mib),
    )(
        *(
            pltpu.with_memory_space_constraint(array, pltpu.HBM)
            for array in (
                pair_orders.reshape(2, PEERS), kappa.reshape(1, NR), right_op, left_op, grid_terms, legendre, state,
            )
        )
    )
    return pl.pallas_call(
        join,
        out_shape=(jax.ShapeDtypeStruct(grid_shape, F32), jax.ShapeDtypeStruct(spectral_shape, BF16)),
        in_specs=[vmem] * 5,
        out_specs=(hbm, hbm),
        scratch_shapes=[
            pltpu.VMEM(grid_shape, F32),
            pltpu.SemaphoreType.DMA((LAT + 1,)),
        ],
        compiler_params=pltpu.CompilerParams(vmem_limit_bytes=16 * mib),
    )(*parts)


def solution(mesh):
    return jax.shard_map(
        on_device,
        mesh=mesh,
        in_specs=(
            P(("row", "col"), "sec", None),
            P(),
            P(("sec", "row", "col"), None, None),
            P(("sec", "row", "col"), None, None),
            P(),
            P(),
            P(),
        ),
        out_specs=(P(("row", "col"), "sec", None), P(("sec", "row", "col"), None, None)),
        check_vma=False,
    )
```

```python
import functools
import math

import jax
import jax.numpy as jnp
from jax import lax
from jax.experimental import pallas as pl
from jax.experimental.pallas import tpu as pltpu
from jax.sharding import PartitionSpec as P

time_step = 0.5
filter_strength = 36.0
MESH = pl.DeviceIdType.MESH
F32 = jnp.float32
BF16 = jnp.bfloat16

LAT = 6
HALF = 768
NR = 128
PEERS = 128
DEG = 512
NTH = 768


GIVE_A0, GIVE_A1, TO_A0, TO_A1, TO_B0, TO_B1, PASS_B0, PASS_B1, SEMS = 0, 4, 5, 6, 7, 8, 12, 13, 17


def ring(count, k):
    return count // 2 + (k + 1) // 2 * (1 - 2 * (k % 2))


def each_peer(row, col, body, first=0, last=16):
    z, y, x = lax.rem(row, 8), 2 * lax.div(row, 8) + lax.div(col, 4), lax.rem(col, 4)
    along = [lax.rem(z + ring(8, k), 8) for k in range(8)]

    def line(i, count):
        x2 = lax.rem(x + ring(4, lax.rem(i, 4)), 4)
        y2 = lax.rem(y + ring(4, lax.div(i, 4)), 4)
        row2, col2 = 8 * lax.div(y2, 2), 4 * lax.rem(y2, 2) + x2
        for z2 in along[:count]:
            body(row2 + z2, col2)

    def step(i, _):
        line(i, 8)
        return 0

    lax.fori_loop(first, min(last, 15), step, 0)
    if last == 16:
        line(jnp.int32(15), 7)


def wave(order, longitude):
    longitudes = 2 * HALF
    phase = order * longitude
    turns = jnp.round(phase * (1.0 / longitudes))
    angle = (phase - turns * longitudes) * (math.pi / longitudes)
    square = angle * angle
    sine = angle * (1.0 + square * (-1 / 6 + square * (1 / 120 + square * (-1 / 5040 + square * (1 / 362880)))))
    cosine = 1.0 + square * (
        -1 / 2 + square * (1 / 24 + square * (-1 / 720 + square * (1 / 40320 - square * (1 / 3628800))))
    )
    scale = 1.0 / math.sqrt(longitudes)
    return scale - (2.0 * scale) * sine * sine, (-2.0 * scale) * sine * cosine


def dot(a, b):
    return jnp.dot(a, b, preferred_element_type=F32)


def kernel(
    orders_hbm, kappa_hbm, right_hbm, left_hbm, grid_hbm, legendre_hbm, state_hbm,
    sum_ref, table_other, other_b0, other_b1, new_ref,
    orders_s, orders_v, kappa, right, left,
    grid, grid_low, table, table_t,
    wide_a0, wide_a1, wide_b0, wide_b1, pack_a0, pack_a1, pack_b0, pack_b1, got_a0, got_a1, got_b0, got_b1,
    give_a0, give_a1, taken_a0, taken_a1, passed_b0, passed_b1,
    legendre, permute, rows, rows_t, state, columns, factor, ends, chosen,
    load_sem, send_sem, recv_sem,
):
    sec, row, col = lax.axis_index("sec"), lax.axis_index("row"), lax.axis_index("col")
    me = 8 * row + col
    partner = (1 - sec, row, col)
    sign = (1 - 2 * sec).astype(F32)

    loads = [pltpu.make_async_copy(orders_hbm, orders_v, load_sem.at[0])]
    loads += [pltpu.make_async_copy(grid_hbm.at[t], grid.at[t], load_sem.at[t + 1]) for t in range(LAT)]
    for source, target in (
        (orders_hbm, orders_s), (legendre_hbm.at[0], legendre), (state_hbm.at[0], state),
        (kappa_hbm, kappa), (right_hbm, right), (left_hbm, left),
    ):
        loads.append(pltpu.make_async_copy(source, target, load_sem.at[len(loads)]))
    for load in loads:
        load.start()

    barrier = pltpu.get_barrier_semaphore()

    def greet(row2, col2):
        pl.semaphore_signal(barrier, inc=1, device_id=(sec, row2, col2), device_id_type=MESH)

    pl.semaphore_signal(barrier, inc=1, device_id=partner, device_id_type=MESH)
    each_peer(row, col, greet)

    loads[0].wait()
    evens = []
    for which in range(2):
        low = orders_v[pl.ds(sec if which == 0 else 1 - sec, 1), :]
        evens.append(jnp.where(lax.rem(low, 2) == 0, low, DEG - 1 - low).astype(F32))

    for which in range(2):
        even_t = jnp.transpose(jnp.broadcast_to(evens[which], (PEERS, PEERS)))
        real, imag = wave(even_t, lax.broadcasted_iota(jnp.int32, (PEERS, 128), 1).astype(F32))
        turn_real, turn_imag = wave(even_t, 128.0)
        turn_real, turn_imag = turn_real * math.sqrt(2 * HALF), turn_imag * math.sqrt(2 * HALF)
        for lane in range(HALF // 128):
            longitude = (lax.broadcasted_iota(jnp.int32, (8, 128), 1) + 128 * lane).astype(F32)
            last_real, last_imag = wave(jnp.full((8, 128), DEG - 1.0, F32), longitude)
            last_real = (last_real * (sign * math.sqrt(2 * HALF)))[:1]
            last_imag = (last_imag * (sign * math.sqrt(2 * HALF)))[:1]
            span = pl.ds(128 * lane, 128)
            table[which, 0:PEERS, span] = real.astype(BF16)
            table[which, PEERS : 2 * PEERS, span] = imag.astype(BF16)
            table[which, 2 * PEERS : 3 * PEERS, span] = (last_real * real + last_imag * imag).astype(BF16)
            table[which, 3 * PEERS :, span] = (last_imag * real - last_real * imag).astype(BF16)
            real, imag = real * turn_real - imag * turn_imag, imag * turn_real + real * turn_imag

    def there(c, parity, t):
        at = 12 * c + 6 * parity + t
        return (wide_a0, pl.ds(at, PEERS, stride=16)) if at < 16 else (wide_a1, pl.ds(at - 16, PEERS, stride=8))

    def narrow(wide, pack, added=None):
        def body(i, _):
            values = wide[pl.ds(256 * i, 256), :].reshape(32, 8, NR)
            if added is not None:
                values = values + added[pl.ds(32 * i, 32)].astype(F32)
            pack[pl.ds(32 * i, 32)] = values.astype(BF16)
            return 0

        lax.fori_loop(0, pack.shape[0] // 32, body, 0)

    for t in range(LAT):
        loads[t + 1].wait()
        grid_low[t] = grid[t].astype(BF16)
    for which in (1, 0):
        for k in range(LAT // 2):
            values = jnp.concatenate([grid_low[2 * k], grid_low[2 * k + 1]], axis=1)
            sums = dot(table[which], values)
            for parity in range(2):
                for c in range(2):
                    for j in range(2):
                        wide, span = there(c, parity, 2 * k + j)
                        at = (2 * parity + c) * PEERS
                        wide[span, :] = sums[at : at + PEERS, j * NR : (j + 1) * NR]
        if which == 1:
            narrow(wide_a0, give_a0)
            narrow(wide_a1, give_a1)

    pl.semaphore_wait(barrier, PEERS)

    def to_partner(source, target, sem):
        return pltpu.make_async_remote_copy(
            source, target, send_sem.at[sem], recv_sem.at[sem], device_id=partner, device_id_type=MESH
        )

    y = 2 * lax.div(row, 8) + lax.div(col, 4)

    def run_of(y2, z):
        return pl.multiple_of(2 * (64 * lax.div(y2, 2) + 4 * lax.rem(y2, 2) + 8 * z), 8)

    def runs(body):
        def step(z, _):
            body(z)
            return 0

        lax.fori_loop(0, 8, step, 0)

    def send_runs(source, target, y2, sem):
        def body(z):
            at = run_of(y2, z)
            to_partner(source.at[pl.ds(at, 8)], target.at[pl.ds(at, 8)], sem).start()

        runs(body)

    def sent_runs(source, target, sem):
        return to_partner(source.at[pl.ds(0, 64)], target.at[pl.ds(0, 64)], sem)

    def widen_runs(got, wide, y2):
        def body(z):
            at = run_of(y2, z)
            wide[pl.ds(8 * at, 64), :] = got[pl.ds(at, 8)].astype(F32).reshape(64, NR)

        runs(body)

    for b in range(4):
        send_runs(give_a0, taken_a0, lax.rem(y + ring(4, b), 4), GIVE_A0 + b)
    to_partner(give_a1, taken_a1, GIVE_A1).start()

    def exchange(pack, got, sem, first=0, last=16):
        tiles = pack.shape[0] // PEERS

        def send(row2, col2):
            pltpu.make_async_remote_copy(
                pack.at[pl.ds(tiles * (8 * row2 + col2), tiles)], got.at[pl.ds(tiles * me, tiles)],
                send_sem.at[sem], recv_sem.at[sem], device_id=(sec, row2, col2), device_id_type=MESH,
            ).start()

        each_peer(row, col, send, first, last)
        if last == 16:
            got[pl.ds(tiles * me, tiles)] = pack[pl.ds(tiles * me, tiles)]

    def whole(pack, got, sem, messages=PEERS - 1):
        count = pack.shape[0] // PEERS * messages
        return to_partner(pack.at[pl.ds(0, count)], got.at[pl.ds(0, count)], sem)

    for b in range(4):
        sent_runs(give_a0, taken_a0, GIVE_A0 + b).wait_recv()

        def add(z):
            at = run_of(lax.rem(y + ring(4, b), 4), z)
            values = wide_a0[pl.ds(8 * at, 64), :].reshape(8, 8, NR) + taken_a0[pl.ds(at, 8)].astype(F32)
            pack_a0[pl.ds(at, 8)] = values.astype(BF16)

        runs(add)
        exchange(pack_a0, got_a0, TO_A0, 4 * b, 4 * b + 4)
    to_partner(give_a1, taken_a1, GIVE_A1).wait_recv()
    narrow(wide_a1, pack_a1, taken_a1)
    exchange(pack_a1, got_a1, TO_A1)

    for load in loads[LAT + 1 :]:
        load.wait()
    for lane in range(HALF // 128):
        longitude = (lax.broadcasted_iota(jnp.int32, (128, PEERS), 0) + 128 * lane).astype(F32)
        span = pl.ds(128 * lane, 128)
        for which in range(2):
            for parity in range(2):
                order = evens[which] if parity == 0 else (DEG - 1.0) - evens[which]
                real, imag = wave(jnp.broadcast_to(order, (128, PEERS)), longitude)
                if parity == 1:
                    real, imag = real * sign, imag * sign
                target = table_t if which == 0 else table_other
                at = PEERS * parity
                target[span, at : at + PEERS] = real.astype(BF16)
                target[span, at + 2 * PEERS : at + 3 * PEERS] = imag.astype(BF16)
    for t in range(LAT):
        latitude = lax.broadcasted_iota(jnp.int32, (NTH, PEERS), 0)
        device = lax.broadcasted_iota(jnp.int32, (NTH, PEERS), 1)
        permute[:, t * PEERS : (t + 1) * PEERS] = jnp.where(latitude == LAT * device + t, 1.0, 0.0).astype(BF16)
    rows[...] = dot(legendre[...], permute[...]).astype(BF16)
    for i in range(4):
        for j in range(LAT):
            rows_t[pl.ds(128 * j, 128), pl.ds(128 * i, 128)] = jnp.transpose(
                rows[pl.ds(128 * i, 128), pl.ds(128 * j, 128)].astype(F32)
            ).astype(BF16)
    ends[...] = jnp.transpose(jnp.broadcast_to(rows[DEG:, :].astype(F32), (128, NTH)))
    mine = orders_s[sec, me]
    index = lax.broadcasted_iota(jnp.int32, (DEG + 1, NR), 0)
    leading = index < DEG - mine
    chosen[...] = jnp.where(leading == (lax.rem(mine, 2) == 0), 1.0, 0.0)
    degree = jnp.where(leading, mine + index, index - 1).astype(F32)
    mode = lax.broadcasted_iota(jnp.int32, (1, NR), 1).astype(F32) * (1.0 / NR)
    mode4 = (mode * mode) * (mode * mode)
    mode8 = mode4 * mode4
    mode16 = mode8 * mode8
    damping = jnp.exp(-filter_strength * (mode16 * mode16 * mode4))
    factor[...] = damping / (1.0 + kappa[...] + degree * (degree + 1.0) * (1.0 / (DEG * DEG)))

    for c in range(2):
        if c == 0:
            whole(pack_a0, got_a0, TO_A0).wait_recv()
            widen(got_a0, wide_a0)
        else:
            whole(pack_a1, got_a1, TO_A1).wait_recv()
            widen(got_a1, wide_a1)
        first = chosen[...] > 0.5
        for parity in range(2):
            for t in range(LAT):
                wide, span = there(c, parity, t)
                columns[t * PEERS : (t + 1) * PEERS, parity * NR : (parity + 1) * NR] = wide[span, :].astype(BF16)
        both = dot(rows[...], columns[...])
        coefficient = jnp.where(first, both[:, :NR], both[:, NR:])
        right_side = state[:, c * NR : (c + 1) * NR].astype(F32) + time_step * coefficient
        scaled = (dot(right_side.astype(BF16), right[...]) * factor[...]).astype(BF16)
        new = dot(scaled, left[...]).astype(BF16)
        new_ref[0, :, c * NR : (c + 1) * NR] = new
        new = new.astype(F32)
        split = jnp.concatenate([jnp.where(first, new, 0.0), jnp.where(first, 0.0, new)], axis=1)
        tail = split[DEG:, :]
        split = split[:DEG, :].astype(BF16)
        for t in range(LAT):
            block = slice(t * PEERS, (t + 1) * PEERS)
            sums = dot(rows_t[block, :], split)
            for parity in range(2):
                wide, span = back(wide_b0, wide_b1, c, parity, t)
                half = slice(parity * NR, (parity + 1) * NR)
                wide[span, :] = sums[:, half] + ends[block, :] * tail[:, half]
        if c == 0:
            narrow(wide_b0, pack_b0)
            exchange(pack_b0, got_b0, TO_B0)
        else:
            for b in range(4):

                def cut(z):
                    at = run_of(lax.rem(y + ring(4, b), 4), z)
                    pack_b1[pl.ds(at, 8)] = wide_b1[pl.ds(8 * at, 64), :].reshape(8, 8, NR).astype(BF16)

                runs(cut)
                exchange(pack_b1, got_b1, TO_B1 + b, 4 * b, 4 * b + 4)

    whole(pack_b0, got_b0, TO_B0).wait_recv()
    to_partner(got_b0, passed_b0, PASS_B0).start()
    widen(got_b0, wide_b0)

    def put_sum(t, value):
        sum_ref[t] = value

    def add_sum(t, value):
        sum_ref[t] = sum_ref[t] + value

    for k in range(2):
        order_sums(wide_b0, wide_b1, table_t, k, (0,), put_sum)
    for b in range(4):
        y2 = lax.rem(y + 4 - ring(4, b), 4)
        whole(pack_b1, got_b1, TO_B1 + b, 32 if b < 3 else 31).wait_recv()
        send_runs(got_b1, passed_b1, y2, PASS_B1 + b)
        widen_runs(got_b1, wide_b1, y2)
        if b == 0:
            to_partner(got_b0, passed_b0, PASS_B0).wait_recv()
            widen(passed_b0, other_b0)
            for k in range(2):
                order_sums(other_b0, other_b1, table_other, k, (0,), add_sum)
        else:
            sent_runs(got_b1, passed_b1, PASS_B1 + b - 1).wait_recv()
            widen_runs(passed_b1, other_b1, lax.rem(y + 4 - ring(4, b - 1), 4))

    for k in range(2):
        order_sums(wide_b0, wide_b1, table_t, k, (1,), add_sum)
    order_sums(wide_b0, wide_b1, table_t, 2, (0, 1), put_sum)

    sent_runs(got_b1, passed_b1, PASS_B1 + 3).wait_recv()
    widen_runs(passed_b1, other_b1, y)
    for b in range(4):
        sent_runs(got_b1, passed_b1, PASS_B1 + b).wait_send()
        whole(pack_b1, got_b1, TO_B1 + b, 32 if b < 3 else 31).wait_send()
        sent_runs(give_a0, taken_a0, GIVE_A0 + b).wait_send()
    to_partner(got_b0, passed_b0, PASS_B0).wait_send()
    whole(pack_b0, got_b0, TO_B0).wait_send()
    whole(pack_a1, got_a1, TO_A1).wait_send()
    whole(pack_a0, got_a0, TO_A0).wait_send()
    to_partner(give_a1, taken_a1, GIVE_A1).wait_send()


def back(wide_b0, wide_b1, c, parity, t):
    if c == 0 and t < 4:
        return wide_b0, pl.ds(4 * parity + t, PEERS, stride=8)
    at = 12 * c - 8 + 6 * parity + t if c == 1 else 2 * parity + t - 4
    return wide_b1, pl.ds(at, PEERS, stride=16)


def widen(got, wide):
    def body(i, _):
        wide[pl.ds(256 * i, 256), :] = got[pl.ds(32 * i, 32)].astype(F32).reshape(256, NR)
        return 0

    lax.fori_loop(0, got.shape[0] // 32, body, 0)


def order_sums(wide_b0, wide_b1, table, k, parts, put):
    halves = []
    for t in (2 * k, 2 * k + 1):
        pieces = []
        for c in parts:
            for parity in range(2):
                wide, span = back(wide_b0, wide_b1, c, parity, t)
                pieces.append(wide[span, :].astype(BF16))
        halves.append(jnp.concatenate(pieces, axis=0))
    columns = slice(2 * PEERS * parts[0], 2 * PEERS * (parts[-1] + 1))
    sums = dot(table[:, columns], jnp.concatenate(halves, axis=1))
    for j in range(2):
        put(2 * k + j, sums[:, j * NR : (j + 1) * NR])


def join(sum_ref, table_ref, wide_b0, wide_b1, new_ref, evolved_hbm, new_hbm, total, sem):
    copies = [pltpu.make_async_copy(new_ref, new_hbm, sem.at[LAT])]
    copies[0].start()

    def put(t, value):
        total[t] = sum_ref[t] + value
        copies.append(pltpu.make_async_copy(total.at[t], evolved_hbm.at[t], sem.at[t]))
        copies[-1].start()

    for k in range(2):
        order_sums(wide_b0, wide_b1, table_ref, k, (1,), put)
    order_sums(wide_b0, wide_b1, table_ref, 2, (0, 1), put)
    for copy in copies:
        copy.wait()


def on_device(grid_terms, pair_orders, legendre, state, kappa, right_op, left_op):
    vmem = pl.BlockSpec(memory_space=pltpu.VMEM)
    hbm = pl.BlockSpec(memory_space=pltpu.HBM)
    mib = 1024 * 1024
    grid_shape = (LAT, HALF, NR)
    spectral_shape = (1, DEG + 1, 2 * NR)

    def tiles_of(count):
        return (count * PEERS, 8, NR)

    parts = pl.pallas_call(
        kernel,
        out_shape=(
            jax.ShapeDtypeStruct(grid_shape, F32),
            jax.ShapeDtypeStruct((HALF, 4 * PEERS), BF16),
            jax.ShapeDtypeStruct((8 * PEERS, NR), F32),
            jax.ShapeDtypeStruct((16 * PEERS, NR), F32),
            jax.ShapeDtypeStruct(spectral_shape, BF16),
        ),
        in_specs=[hbm] * 7,
        out_specs=(vmem,) * 5,
        scratch_shapes=[
            pltpu.SMEM((2, PEERS), jnp.int32),
            pltpu.VMEM((2, PEERS), jnp.int32),
            pltpu.VMEM((1, NR), F32),
            pltpu.VMEM((NR, NR), BF16),
            pltpu.VMEM((NR, NR), BF16),
            pltpu.VMEM(grid_shape, F32),
            pltpu.VMEM(grid_shape, BF16),
            pltpu.VMEM((2, 4 * PEERS, HALF), BF16),
            pltpu.VMEM((HALF, 4 * PEERS), BF16),
        ]
        + [pltpu.VMEM((count * 8 * PEERS, NR), F32) for count in (2, 1, 1, 2)]
        + [pltpu.VMEM(tiles_of(count), BF16) for count in (2, 1, 1, 2, 2, 1, 1, 2, 2, 1, 2, 1, 1, 2)]
        + [
            pltpu.VMEM((DEG + 1, NTH), BF16),
            pltpu.VMEM((NTH, NTH), BF16),
            pltpu.VMEM((DEG + 1, NTH), BF16),
            pltpu.VMEM((NTH, DEG), BF16),
            pltpu.VMEM((DEG + 1, 2 * NR), BF16),
            pltpu.VMEM((NTH, 2 * NR), BF16),
            pltpu.VMEM((DEG + 1, NR), F32),
            pltpu.VMEM((NTH, NR), F32),
            pltpu.VMEM((DEG + 1, NR), F32),
            pltpu.SemaphoreType.DMA((LAT + 7,)),
            pltpu.SemaphoreType.DMA((SEMS,)),
            pltpu.SemaphoreType.DMA((SEMS,)),
        ],
        compiler_params=pltpu.CompilerParams(collective_id=0, has_side_effects=True, vmem_limit_bytes=36 * mib),
    )(
        *(
            pltpu.with_memory_space_constraint(array, pltpu.HBM)
            for array in (
                pair_orders.reshape(2, PEERS), kappa.reshape(1, NR), right_op, left_op, grid_terms, legendre, state,
            )
        )
    )
    return pl.pallas_call(
        join,
        out_shape=(jax.ShapeDtypeStruct(grid_shape, F32), jax.ShapeDtypeStruct(spectral_shape, BF16)),
        in_specs=[vmem] * 5,
        out_specs=(hbm, hbm),
        scratch_shapes=[
            pltpu.VMEM(grid_shape, F32),
            pltpu.SemaphoreType.DMA((LAT + 1,)),
        ],
        compiler_params=pltpu.CompilerParams(vmem_limit_bytes=16 * mib),
    )(*parts)


def solution(mesh):
    return jax.shard_map(
        on_device,
        mesh=mesh,
        in_specs=(
            P(("row", "col"), "sec", None),
            P(),
            P(("sec", "row", "col"), None, None),
            P(("sec", "row", "col"), None, None),
            P(),
            P(),
            P(),
        ),
        out_specs=(P(("row", "col"), "sec", None), P(("sec", "row", "col"), None, None)),
        check_vma=False,
    )
```
